256 devices in a mesh: row: 32 (over x_lo, z, core), col: 8 (over y, x_hi).
Axes of the slice: x: 4 (x_hi: 2, x_lo: 2; x = x_hi * 2 + x_lo), y: 4, z: 8, core: 2. Of those that a mesh axis runs over, the one named last changes fastest.
Arguments:
- corr: float32 [2, 8192, 8192], P(None, 'row', 'col'), may hold values from -6 to 6
- slope_prev: float32 [2, 8192, 8192], P(None, 'row', 'col'), may hold values from -6 to 6
- kappa: float32 [8192], replicated, may hold values from 0.05 to 0.2
- detuning: float32 [8192], replicated, may hold values from -1 to 1
- pump: float32 [8192], replicated, may hold values from 0.5 to 2
- round_trip: float32 [2], replicated, may hold values from -0.6 to 0.6
Outputs:
- slope: float32 [2, 8192, 8192], P(None, 'row', 'col')
The draws below stay inside these ranges and needn't reach their ends.
All inputs are finite; a program needn't handle non-finite values.
Results may differ from the reference program's by a relative error of at most 0.00005.
Values sent between devices are 32-bit elements; how exact they have to be, the bound alone decides.
No kernel may reach another device: no remote copies, remote signals or barrier semaphores. Data moves between devices by JAX's collectives and lax.ppermute only.
A program may use at most 64 MiB of HBM per device.

```python
import math
import jax
import jax.numpy as jnp

N = 8192


def shard_levels(stream_key, shape, shards, smallest, top_value):
    level, own = 1.0, jax.random.fold_in(stream_key, 6)
    for position, parts in shards:
        heights = jnp.exp(jax.random.uniform(jax.random.fold_in(own, position), (parts,), jnp.float32, smallest / len(shards), top_value / len(shards)))
        level = level * jnp.repeat(heights, shape[position] // parts).reshape([-1 if axis == position else 1 for axis in range(len(shape))])
    return level


def noise(stream_key, dims, spread, limit, cuts=(), kind=jnp.bfloat16):
    values = spread * jax.random.normal(stream_key, dims, jnp.float32)
    if cuts:
        values = values * shard_levels(stream_key, dims, cuts, -0.22, 0.18)
    return jnp.clip(values, -limit, limit).astype(kind)


def setup_inputs(seed: int = 0) -> dict:
    key_list = jax.random.split(jax.random.key(seed), 7)
    return {
        "corr": noise(key_list[0], (2, N, N), 1.0, 6.0, ((1, 32), (2, 8)), jnp.float32),
        "slope_prev": noise(key_list[1], (2, N, N), 1.0, 6.0, ((1, 32), (2, 8)), jnp.float32),
        "kappa": jnp.clip(jnp.exp(jax.random.uniform(key_list[2], (N,), jnp.float32, math.log(0.05), math.log(0.2))), 0.05, 0.2),
        "detuning": jnp.clip(jax.random.uniform(key_list[3], (N,), jnp.float32, -1.0, 1.0), -1.0, 1.0),
        "pump": jnp.clip(jax.random.uniform(key_list[4], (N,), jnp.float32, 0.5, 2.0), 0.5, 2.0),
        "round_trip": jnp.clip(jax.random.uniform(key_list[5], (2,), jnp.float32, -0.6, 0.6), -0.6, 0.6),
    }


def reference(corr, slope_prev, kappa, detuning, pump, round_trip):
    section = corr + 0.25 * slope_prev
    rho_re = round_trip[0]
    rho_im = round_trip[1]
    upper = section * kappa[None, :, None]
    inclusive = jnp.cumsum(upper, axis=1)
    before = inclusive - upper
    after = inclusive[:, -1:, :] - inclusive
    turned = jnp.stack([rho_re * after[0] - rho_im * after[1], rho_re * after[1] + rho_im * after[0]])
    field_left = -kappa[None, :, None] * (before + 0.5 * upper + turned)
    weighted = section * kappa[None, None, :]
    inclusive = jnp.cumsum(weighted, axis=2)
    before = inclusive - weighted
    after = inclusive[:, :, -1:] - inclusive
    turned = jnp.stack([rho_re * after[0] + rho_im * after[1], rho_re * after[1] - rho_im * after[0]])
    field_right = -kappa[None, None, :] * (before + 0.5 * weighted + turned)
    gap = detuning[None, :] - detuning[:, None]
    spin = jnp.stack([-gap * section[1], gap * section[0]])
    slope = field_left + field_right + spin
    index = jnp.arange(kappa.shape[0], dtype=jnp.int32)
    slope = slope.at[0, index, index].add(pump)
    return slope
```

```python
import itertools

import jax
import jax.numpy as jnp
from jax import lax
from jax.experimental import pallas as pl
from jax.experimental.pallas import tpu as pltpu
from jax.sharding import Mesh, PartitionSpec as P

AXES = ("xl", "z", "core", "y", "xh")
SIZES = (2, 8, 2, 4, 2)
ROW = AXES[:3]
COL = AXES[3:]
PLACES = [dict(zip(AXES, place)) for place in itertools.product(*map(range, SIZES))]


LANES = 128
CHUNKS = 8
BLOCK = 256
MIB = 1 << 20


def flat(place):
    index = 0
    for axis, size in zip(AXES, SIZES):
        index = index * size + place[axis]
    return index


def swap(x, axis, partner):
    pairs = [(flat(p), flat({**p, axis: partner(p[axis])})) for p in PLACES]
    return lax.ppermute(x, AXES, pairs)


def across(i):
    return i ^ 1


def z_next(z):
    return (z + 1) % 8 if z % 2 else (z - 1) % 8


Z_FAR = (3, 6, 5, 0, 7, 2, 1, 4)


def z_far(z):
    return Z_FAR[z]


def y_next(y):
    return (y + 1) % 4 if y % 2 else (y - 1) % 4


def spot():
    row = (lax.axis_index("xl") * 8 + lax.axis_index("z")) * 2 + lax.axis_index("core")
    col = lax.axis_index("y") * 2 + lax.axis_index("xh")
    return row, col


def down_rows(ref, row):
    halves = []
    for half in range(2):
        lanes = ref[pl.ds(row * 2 + half, 1), :]
        halves.append(jnp.broadcast_to(lanes, (LANES, LANES)).T)
    return jnp.concatenate(halves, axis=0)


def sums_kernel(
    corr_hbm, slope_hbm, kappa_hbm, detune_hbm, pump_hbm,
    sec_ref, rows_ref, cols_ref, kappa_ref, detune_ref, pump_ref,
    corr_buf, slope_buf, kap_rows, col_part, big_sems, small_sems,
):
    row, col = spot()
    height = 256 // CHUNKS
    small = [
        pltpu.make_async_copy(kappa_hbm, kappa_ref, small_sems.at[0]),
        pltpu.make_async_copy(detune_hbm, detune_ref, small_sems.at[1]),
        pltpu.make_async_copy(pump_hbm, pump_ref, small_sems.at[2]),
    ]
    small[0].start()
    copies = []
    for c in range(CHUNKS):
        part = pl.ds(c * height, height)
        pair = (
            pltpu.make_async_copy(corr_hbm.at[:, part], corr_buf.at[:, part], big_sems.at[0, c]),
            pltpu.make_async_copy(slope_hbm.at[:, part], slope_buf.at[:, part], big_sems.at[1, c]),
        )
        for copy in pair:
            copy.start()
        copies.append(pair)
    small[1].start()
    small[2].start()
    small[0].wait()
    kap_rows[...] = down_rows(kappa_ref, row)
    kap_cols = [
        jnp.broadcast_to(kappa_ref[pl.ds(col * 8 + b, 1), :], (8, LANES)) for b in range(8)
    ]
    totals = [jnp.zeros((8, LANES), jnp.float32) for _ in range(16)]
    for c in range(CHUNKS):
        for copy in copies[c]:
            copy.wait()

        def group(g, totals):
            totals = list(totals)
            at = pl.ds(pl.multiple_of(c * height + g * 8, 8), 8)
            kr = kap_rows[at, :]
            for p in range(2):
                along = None
                for b in range(8):
                    lanes = pl.ds(b * LANES, LANES)
                    s = corr_buf[p, at, lanes] + 0.25 * slope_buf[p, at, lanes]
                    sec_ref[p, at, lanes] = s
                    totals[p * 8 + b] = totals[p * 8 + b] + s * kr
                    w = s * kap_cols[b]
                    along = w if along is None else along + w
                col_part[p, at, :] = along
            return tuple(totals)

        totals = lax.fori_loop(0, height // 8, group, tuple(totals), unroll=True)
    for p in range(2):
        for b in range(8):
            rows_ref[pl.ds(p, 1), pl.ds(b * LANES, LANES)] = jnp.sum(
                totals[p * 8 + b], axis=0, keepdims=True
            )
        summed = lax.dot_general(
            jnp.ones((8, LANES), jnp.float32), col_part[p],
            (((1,), (1,)), ((), ())),
            precision=lax.Precision.HIGHEST, preferred_element_type=jnp.float32,
        )
        cols_ref[pl.ds(p, 1), :] = summed[0:1, :]
    small[1].wait()
    small[2].wait()


def split(x):
    high = x.astype(jnp.bfloat16)
    return high, (x - high.astype(jnp.float32)).astype(jnp.bfloat16)


def table(lower):
    a = lax.broadcasted_iota(jnp.int32, (BLOCK, BLOCK), 0)
    b = lax.broadcasted_iota(jnp.int32, (BLOCK, BLOCK), 1)
    before = (b < a) if lower else (a < b)
    return jnp.where(before, 1.0, jnp.where(a == b, 0.5, 0.0)).astype(jnp.bfloat16)


def matmul(a, b):
    return jnp.dot(a, b, preferred_element_type=jnp.float32)


def twice(x):
    return jnp.concatenate([x, x], axis=1)


def along_lanes(ref, first):
    return jnp.concatenate([ref[pl.ds(first, 1), :], ref[pl.ds(first + 1, 1), :]], axis=1)


def rows_kernel(rho_ref, sec_ref, kappa_ref, detune_ref, pump_ref, base_ref):
    row, col = spot()
    rho_re, rho_im = rho_ref[0], rho_ref[1]
    e, f = 1.0 - rho_re, -rho_im
    kr = twice(down_rows(kappa_ref, row))
    dr = twice(down_rows(detune_ref, row))
    pr = twice(down_rows(pump_ref, row))
    mre_r = (0.5 * rho_re) * kr * kr
    mim_r = (0.5 * rho_im) * kr * kr - dr
    lower = table(True)
    for b in range(1024 // BLOCK):
        lanes = pl.ds(b * BLOCK, BLOCK)
        kc = along_lanes(kappa_ref, col * 8 + 2 * b)
        dc = along_lanes(detune_ref, col * 8 + 2 * b)
        q = []
        for p in range(2):
            high, low = split(sec_ref[p, :, lanes] * kr)
            q.append(matmul(lower, high) + matmul(lower, low))
        s_re, s_im = sec_ref[0, :, lanes], sec_ref[1, :, lanes]
        m_re = mre_r + (0.5 * rho_re) * kc * kc
        m_im = mim_r + (dc - (0.5 * rho_im) * kc * kc)
        i = lax.broadcasted_iota(jnp.int32, (256, BLOCK), 0) + row * 256
        k = lax.broadcasted_iota(jnp.int32, (256, BLOCK), 1) + (col * 1024 + b * BLOCK)
        base_ref[0, :, lanes] = (
            m_re * s_re - m_im * s_im - kr * (e * q[0] - f * q[1]) + jnp.where(i == k, pr, 0.0)
        )
        base_ref[1, :, lanes] = m_re * s_im + m_im * s_re - kr * (e * q[1] + f * q[0])


def cols_kernel(rho_ref, sec_ref, kappa_ref, part_ref, base_ref):
    _, col = spot()
    e, f = 1.0 - rho_ref[0], rho_ref[1]
    upper = table(False)
    carry = [jnp.zeros((256, 1), jnp.float32) for _ in range(2)]
    for b in range(1024 // BLOCK):
        lanes = pl.ds(b * BLOCK, BLOCK)
        kc = along_lanes(kappa_ref, col * 8 + 2 * b)
        q = []
        for p in range(2):
            w = sec_ref[p, :, lanes] * kc
            high, low = split(w)
            q.append(matmul(high, upper) + matmul(low, upper) + carry[p])
            carry[p] = carry[p] + jnp.sum(w, axis=1, keepdims=True)
        base_ref[0, :, lanes] = part_ref[0, :, lanes] - kc * (e * q[0] - f * q[1])
        base_ref[1, :, lanes] = part_ref[1, :, lanes] - kc * (e * q[1] + f * q[0])


def last_kernel(
    rho_ref, kappa_ref, base_ref, row_b, row_a, col_b, col_a,
    out_hbm, out_buf, kap_rows, row_d, col_d, sems,
):
    row, col = spot()
    rho_re, rho_im = rho_ref[0], rho_ref[1]
    height = 256 // CHUNKS
    kap_rows[...] = down_rows(kappa_ref, row)
    b0, b1, a0, a1 = row_b[0:1], row_b[1:2], row_a[0:1], row_a[1:2]
    row_d[0:1] = b0 + (rho_re * a0 - rho_im * a1)
    row_d[1:2] = b1 + (rho_re * a1 + rho_im * a0)
    b0, b1, a0, a1 = col_b[0:1], col_b[1:2], col_a[0:1], col_a[1:2]
    for p, d in enumerate((b0 + (rho_re * a0 + rho_im * a1), b1 + (rho_re * a1 - rho_im * a0))):
        for half in range(2):
            lanes = d[:, half * LANES : (half + 1) * LANES]
            col_d[p, pl.ds(half * LANES, LANES), :] = jnp.broadcast_to(lanes, (LANES, LANES)).T
    kap_cols = [
        jnp.broadcast_to(kappa_ref[pl.ds(col * 8 + b, 1), :], (8, LANES)) for b in range(8)
    ]
    copies = []
    for c in range(CHUNKS):

        def group(g, carry):
            at = pl.ds(pl.multiple_of(c * height + g * 8, 8), 8)
            kr = kap_rows[at, :]
            for p in range(2):
                dc = col_d[p, at, :]
                for b in range(8):
                    lanes = pl.ds(b * LANES, LANES)
                    out_buf[p, at, lanes] = base_ref[p, at, lanes] - (
                        kr * row_d[pl.ds(p, 1), lanes] + kap_cols[b] * dc
                    )
            return carry

        lax.fori_loop(0, height // 8, group, 0, unroll=True)
        part = pl.ds(c * height, height)
        copy = pltpu.make_async_copy(out_buf.at[:, part], out_hbm.at[:, part], sems.at[c])
        copy.start()
        copies.append(copy)
    for copy in copies:
        copy.wait()


VM = pl.BlockSpec(memory_space=pltpu.VMEM)
SM = pl.BlockSpec(memory_space=pltpu.SMEM)
HB = pl.BlockSpec(memory_space=pltpu.HBM)
F32 = jnp.float32


def call(kernel, outs, ins, out_specs, scratch=(), alias={}, flops=0, limit=20):
    return pl.pallas_call(
        kernel,
        out_shape=outs,
        in_specs=ins,
        out_specs=out_specs,
        scratch_shapes=list(scratch),
        input_output_aliases=alias,
        cost_estimate=pl.CostEstimate(flops=flops, bytes_accessed=6 * MIB, transcendentals=0),
        compiler_params=pltpu.CompilerParams(vmem_limit_bytes=limit * MIB),
    )


def vmem(*shape):
    return pltpu.VMEM(shape, F32)


def sums(corr, slope, *small):
    whole = (2, 256, 1024)
    dma = pltpu.SemaphoreType.DMA
    return call(
        sums_kernel,
        [vmem(*whole), vmem(2, 1024), vmem(2, 256)] + [vmem(64, 128)] * 3,
        [HB] * 5,
        [VM] * 6,
        [vmem(*whole), vmem(*whole), vmem(256, 128), vmem(2, 256, 128), dma((2, CHUNKS)), dma((3,))],
    )(corr, slope, *small)


def rows_part(rho, sec, kappa, detune, pump):
    return call(rows_kernel, vmem(2, 256, 1024), [SM] + [VM] * 4, VM, flops=10**9)(
        rho, sec, kappa, detune, pump
    )


def cols_part(rho, sec, kappa, part):
    return call(
        cols_kernel, vmem(2, 256, 1024), [SM] + [VM] * 3, VM, alias={3: 0}, flops=10**9
    )(rho, sec, kappa, part)


def last(rho, kappa, base, *ends):
    whole = (2, 256, 1024)
    return call(
        last_kernel,
        jax.ShapeDtypeStruct(whole, F32),
        [SM] + [VM] * 6,
        HB,
        [vmem(*whole), vmem(256, 128), vmem(2, 1024), vmem(2, 256, 128), pltpu.SemaphoreType.DMA((CHUNKS,))],
    )(rho, kappa, base, *ends)


def put(before, after, lower, x):
    return before + jnp.where(lower, x, 0.0), after + jnp.where(lower, 0.0, x)


def row_ends(own):
    z, core, xl = (lax.axis_index(a) for a in ("z", "core", "xl"))
    before, after = jnp.zeros_like(own), own
    got = swap(own, "core", across)
    before, after = put(before, after, core == 1, got)
    chip = own + got
    got = swap(chip, "z", across)
    before, after = put(before, after, z % 2 == 1, got)
    pair = chip + got
    got = swap(pair, "z", z_next)
    before, after = put(before, after, (z % 2 == 0) & (z != 0) | (z == 7), got)
    far = swap(jnp.stack([pair, got]), "z", z_far)
    before, after = put(before, after, (z == 3) | (z >= 5), far[0])
    before, after = put(before, after, z >= 4, far[1])
    line = pair + got + far[0] + far[1]
    got = swap(line, "xl", across)
    return put(before, after, xl == 1, got)


def col_ends(own):
    y, xh = (lax.axis_index(a) for a in ("y", "xh"))
    before, after = jnp.zeros_like(own), own
    got = swap(own, "xh", across)
    before, after = put(before, after, xh == 1, got)
    place = own + got
    got = swap(place, "y", across)
    before, after = put(before, after, y % 2 == 1, got)
    pair = place + got
    got = swap(pair, "y", y_next)
    return put(before, after, y >= 2, got)


def shards(corr, slope_prev, kappa, detuning, pump, round_trip):
    lines = [v.reshape(64, 128) for v in (kappa, detuning, pump)]
    corr, slope_prev, *lines = (
        pltpu.with_memory_space_constraint(v, pltpu.HBM) for v in (corr, slope_prev, *lines)
    )
    sec, own_rows, own_cols, kappa, detune, pump = sums(corr, slope_prev, *lines)
    row_b, row_a = row_ends(own_rows)
    col_b, col_a = col_ends(own_cols)
    base = rows_part(round_trip, sec, kappa, detune, pump)
    base = cols_part(round_trip, sec, kappa, base)
    return last(round_trip, kappa, base, row_b, row_a, col_b, col_a)


def solution(mesh):
    fine = Mesh(mesh.devices.reshape(SIZES), AXES)
    placed = P(None, ROW, COL)
    return jax.shard_map(
        shards,
        mesh=fine,
        in_specs=(placed, placed, P(), P(), P(), P()),
        out_specs=placed,
        check_vma=False,
    )
```

```python
import itertools

import jax
import jax.numpy as jnp
from jax import lax
from jax.experimental import pallas as pl
from jax.experimental.pallas import tpu as pltpu
from jax.sharding import Mesh, PartitionSpec as P

AXES = ("xl", "z", "core", "y", "xh")
SIZES = (2, 8, 2, 4, 2)
ROW = AXES[:3]
COL = AXES[3:]
PLACES = [dict(zip(AXES, place)) for place in itertools.product(*map(range, SIZES))]


LANES = 128
BLOCK = 256
MIB = 1 << 20


def flat(place):
    index = 0
    for axis, size in zip(AXES, SIZES):
        index = index * size + place[axis]
    return index


def swap(x, **partners):
    pairs = [
        (flat(p), flat({**p, **{axis: partner(p[axis]) for axis, partner in partners.items()}}))
        for p in PLACES
    ]
    return lax.ppermute(x, AXES, pairs)


def across(i):
    return i ^ 1


def z_next(z):
    return (z + 1) % 8 if z % 2 else (z - 1) % 8


def z_far(z):
    return (3, 6, 5, 0, 7, 2, 1, 4)[z]


def y_next(y):
    return (y + 1) % 4 if y % 2 else (y - 1) % 4


def spot():
    row = (lax.axis_index("xl") * 8 + lax.axis_index("z")) * 2 + lax.axis_index("core")
    col = lax.axis_index("y") * 2 + lax.axis_index("xh")
    return row, col


def down_rows(ref, row):
    halves = []
    for half in range(2):
        lanes = ref[pl.ds(row * 2 + half, 1), :]
        halves.append(jnp.broadcast_to(lanes, (LANES, LANES)).T)
    return jnp.concatenate(halves, axis=0)


EDGES = (0, 64, 128, 192, 224, 256)


def sums_kernel(
    corr_hbm, slope_hbm, kappa_hbm, detune_hbm, pump_hbm,
    sec_ref, rows_ref, cols_ref, kap_rows, kappa_buf, detune_ref, pump_ref,
    corr_buf, slope_buf, col_part, sems, small_sems,
):
    row, col = spot()
    kappa_copy, *late = [
        pltpu.make_async_copy(there, here, small_sems.at[n])
        for n, (there, here) in enumerate(
            ((kappa_hbm, kappa_buf), (detune_hbm, detune_ref), (pump_hbm, pump_ref))
        )
    ]
    kappa_copy.start()
    copies = []
    for c, (lo, hi) in enumerate(zip(EDGES, EDGES[1:])):
        part = pl.ds(lo, hi - lo)
        pair = (
            pltpu.make_async_copy(corr_hbm.at[:, part], corr_buf.at[:, part], sems.at[0, c]),
            pltpu.make_async_copy(slope_hbm.at[:, part], slope_buf.at[:, part], sems.at[1, c]),
        )
        for copy in pair:
            copy.start()
        copies.append(pair)
    for copy in late:
        copy.start()
    kappa_copy.wait()
    kap_rows[...] = down_rows(kappa_buf, row)
    kap_cols = [
        jnp.broadcast_to(kappa_buf[pl.ds(col * 8 + b, 1), :], (8, LANES)) for b in range(8)
    ]
    totals = tuple(jnp.zeros((8, LANES), jnp.float32) for _ in range(16))
    for c, (lo, hi) in enumerate(zip(EDGES, EDGES[1:])):
        for copy in copies[c]:
            copy.wait()

        def group(g, totals):
            totals = list(totals)
            at = pl.ds(pl.multiple_of(lo + g * 8, 8), 8)
            kr = kap_rows[at, :]
            for p in range(2):
                along = None
                for b in range(8):
                    lanes = pl.ds(b * LANES, LANES)
                    s = corr_buf[p, at, lanes] + 0.25 * slope_buf[p, at, lanes]
                    sec_ref[p, at, lanes] = s
                    totals[p * 8 + b] = totals[p * 8 + b] + s * kr
                    w = s * kap_cols[b]
                    along = w if along is None else along + w
                col_part[p, at, :] = along
            return tuple(totals)

        totals = lax.fori_loop(0, (hi - lo) // 8, group, totals, unroll=2)
    for p in range(2):
        for b in range(8):
            total = jnp.sum(totals[p * 8 + b], axis=0, keepdims=True)
            rows_ref[pl.ds(p, 1), pl.ds(b * LANES, LANES)] = total
        for half in range(2):
            at = pl.ds(half * LANES, LANES)
            cols_ref[pl.ds(p, 1), at] = jnp.sum(col_part[p, at, :].T, axis=0, keepdims=True)
    for copy in late:
        copy.wait()


def split(x):
    high = x.astype(jnp.bfloat16)
    return high, (x - high.astype(jnp.float32)).astype(jnp.bfloat16)


def table(lower):
    a = lax.broadcasted_iota(jnp.int32, (BLOCK, BLOCK), 0)
    b = lax.broadcasted_iota(jnp.int32, (BLOCK, BLOCK), 1)
    before = (b < a) if lower else (a < b)
    return jnp.where(before, 1.0, jnp.where(a == b, 0.5, 0.0)).astype(jnp.bfloat16)


def matmul(a, b):
    return jnp.dot(a, b, preferred_element_type=jnp.float32)


def twice(x):
    return jnp.concatenate([x, x], axis=1)


def along_lanes(ref, first):
    return jnp.concatenate([ref[pl.ds(first, 1), :], ref[pl.ds(first + 1, 1), :]], axis=1)


def rows_kernel(rho_ref, sec_ref, kap_rows, kappa_ref, detune_ref, pump_ref, base_ref, rho_out):
    row, col = spot()
    rho_re, rho_im = rho_ref[0], rho_ref[1]
    rho_out[0] = jnp.full((8, LANES), rho_re)
    rho_out[1] = jnp.full((8, LANES), rho_im)
    e, f = 1.0 - rho_re, -rho_im
    kr = twice(kap_rows[...])
    dr = twice(down_rows(detune_ref, row))
    pr = twice(down_rows(pump_ref, row))
    mre_r = (0.5 * rho_re) * kr * kr
    mim_r = (0.5 * rho_im) * kr * kr - dr
    lower = table(True)
    for b in range(1024 // BLOCK):
        lanes = pl.ds(b * BLOCK, BLOCK)
        kc = along_lanes(kappa_ref, col * 8 + 2 * b)
        dc = along_lanes(detune_ref, col * 8 + 2 * b)
        q = []
        for p in range(2):
            high, low = split(sec_ref[p, :, lanes] * kr)
            q.append(matmul(lower, high) + matmul(lower, low))
        s_re, s_im = sec_ref[0, :, lanes], sec_ref[1, :, lanes]
        m_re = mre_r + (0.5 * rho_re) * kc * kc
        m_im = mim_r + (dc - (0.5 * rho_im) * kc * kc)
        i = lax.broadcasted_iota(jnp.int32, (256, BLOCK), 0) + row * 256
        k = lax.broadcasted_iota(jnp.int32, (256, BLOCK), 1) + (col * 1024 + b * BLOCK)
        base_ref[0, :, lanes] = (
            m_re * s_re - m_im * s_im - kr * (e * q[0] - f * q[1]) + jnp.where(i == k, pr, 0.0)
        )
        base_ref[1, :, lanes] = m_re * s_im + m_im * s_re - kr * (e * q[1] + f * q[0])


def cols_kernel(rho_ref, sec_ref, kappa_ref, part_ref, base_ref):
    _, col = spot()
    e, f = 1.0 - rho_ref[0], rho_ref[1]
    upper = table(False)
    carry = [jnp.zeros((256, 1), jnp.float32) for _ in range(2)]
    for b in range(1024 // BLOCK):
        lanes = pl.ds(b * BLOCK, BLOCK)
        kc = along_lanes(kappa_ref, col * 8 + 2 * b)
        q = []
        for p in range(2):
            w = sec_ref[p, :, lanes] * kc
            high, low = split(w)
            q.append(matmul(high, upper) + matmul(low, upper) + carry[p])
            carry[p] = carry[p] + jnp.sum(w, axis=1, keepdims=True)
        base_ref[0, :, lanes] = part_ref[0, :, lanes] - kc * (e * q[0] - f * q[1])
        base_ref[1, :, lanes] = part_ref[1, :, lanes] - kc * (e * q[1] + f * q[0])


def carried(rho_ref, before, after, lanes, sign, height):
    rho_re, rho_im = rho_ref[0, 0:1, :], sign * rho_ref[1, 0:1, :]
    b, a = before[:, lanes], after[:, lanes]
    both = b[0:1] + (rho_re * a[0:1] - rho_im * a[1:2]), b[1:2] + (rho_re * a[1:2] + rho_im * a[0:1])
    return [jnp.broadcast_to(x, (height, LANES)) for x in both]


def lines_kernel(rho_ref, before, after, down_ref):
    for half in range(2):
        at = pl.ds(half * LANES, LANES)
        for p, x in enumerate(carried(rho_ref, before, after, at, -1.0, LANES)):
            down_ref[p, at, :] = x.T


OUT_EDGES = (0, 32, 64, 128, 192, 224, 256)


def last_kernel(
    rho_ref, kappa_ref, kap_rows, base_ref, before, after, col_d, out_hbm, out_buf, sems
):
    _, col = spot()
    kap_cols = [
        jnp.broadcast_to(kappa_ref[pl.ds(col * 8 + b, 1), :], (8, LANES)) for b in range(8)
    ]
    row_ds = [
        carried(rho_ref, before, after, pl.ds(b * LANES, LANES), 1.0, 8) for b in range(8)
    ]
    copies = []
    for c, (lo, hi) in enumerate(zip(OUT_EDGES, OUT_EDGES[1:])):

        def group(g, carry):
            at = pl.ds(pl.multiple_of(lo + g * 8, 8), 8)
            kr = kap_rows[at, :]
            for p in range(2):
                dc = col_d[p, at, :]
                for b in range(8):
                    lanes = pl.ds(b * LANES, LANES)
                    out_buf[p, at, lanes] = base_ref[p, at, lanes] - (
                        kr * row_ds[b][p] + kap_cols[b] * dc
                    )
            return carry

        lax.fori_loop(0, (hi - lo) // 8, group, 0, unroll=2)
        part = pl.ds(lo, hi - lo)
        copy = pltpu.make_async_copy(out_buf.at[:, part], out_hbm.at[:, part], sems.at[c])
        copy.start()
        copies.append(copy)
    for copy in copies:
        copy.wait()


VM = pl.BlockSpec(memory_space=pltpu.VMEM)
SM = pl.BlockSpec(memory_space=pltpu.SMEM)
HB = pl.BlockSpec(memory_space=pltpu.HBM)
F32 = jnp.float32


def call(kernel, outs, ins, out_specs, scratch=(), alias={}, flops=0, limit=20):
    return pl.pallas_call(
        kernel,
        out_shape=outs,
        in_specs=ins,
        out_specs=out_specs,
        scratch_shapes=list(scratch),
        input_output_aliases=alias,
        cost_estimate=pl.CostEstimate(flops=flops, bytes_accessed=6 * MIB, transcendentals=0),
        compiler_params=pltpu.CompilerParams(vmem_limit_bytes=limit * MIB),
    )


def vmem(*shape):
    return pltpu.VMEM(shape, F32)


WHOLE = (2, 256, 1024)
DMA = pltpu.SemaphoreType.DMA


def sums(corr, slope, *small):
    return call(
        sums_kernel,
        [vmem(*WHOLE), vmem(2, 1024), vmem(2, 256), vmem(256, 128)] + [vmem(64, 128)] * 3,
        [HB] * 5,
        [VM] * 7,
        [vmem(*WHOLE), vmem(*WHOLE), vmem(2, 256, 128), DMA((2, len(EDGES) - 1)), DMA((3,))],
    )(corr, slope, *small)


def rows_part(rho, sec, kap_rows, *small):
    return call(
        rows_kernel, [vmem(*WHOLE), vmem(2, 8, 128)], [SM] + [VM] * 5, [VM] * 2, flops=10**9
    )(rho, sec, kap_rows, *small)


def cols_part(rho, sec, kappa, part):
    return call(cols_kernel, vmem(*WHOLE), [SM] + [VM] * 3, VM, alias={3: 0}, flops=10**9)(
        rho, sec, kappa, part
    )


def lines(rho, before, after):
    return call(lines_kernel, vmem(2, 256, 128), [VM] * 3, VM, limit=4)(rho, before, after)


def last(*operands):
    return call(
        last_kernel,
        jax.ShapeDtypeStruct(WHOLE, F32),
        [VM] * 7,
        HB,
        [vmem(*WHOLE), DMA((len(OUT_EDGES) - 1,))],
    )(*operands)


def put(before, after, lower, x):
    return before + jnp.where(lower, x, 0.0), after + jnp.where(lower, 0.0, x)


def row_quad(own):
    core, xl = lax.axis_index("core"), lax.axis_index("xl")
    beside = swap(own, core=across)
    ahead, both = swap(own, xl=across), swap(own, xl=across, core=across)
    other = ahead + both
    ends = put(jnp.zeros_like(own), own, core == 1, beside)
    return jnp.stack([own + beside, other]), put(*ends, xl == 1, other)


def row_step(sums, ends, partner, lower):
    got = swap(sums, z=partner)
    ends = put(*put(*ends, lower, got[0]), lax.axis_index("xl") == 1, got[1])
    return got, ends


def row_ends(pair, next_pair, ends):
    z, xl = lax.axis_index("z"), lax.axis_index("xl")
    there = put(jnp.zeros_like(pair[0]), jnp.zeros_like(pair[0]), (z <= 2) | (z == 4), pair[0])
    there = put(*there, (z == 1) | (z == 2) | (z == 4) | (z == 7), next_pair[0])
    there = put(*there, xl == 1, pair[1] + next_pair[1])
    got = swap(jnp.stack(there), z=z_far)
    return ends[0] + got[0], ends[1] + got[1]


def col_pair(own):
    got = swap(own, y=across)
    zero = jnp.zeros_like(own)
    return own + got, put(zero, zero, lax.axis_index("y") % 2 == 1, got)


def col_line(pair, ends):
    return put(*ends, lax.axis_index("y") >= 2, swap(pair, y=y_next))


def col_ends(own, ends):
    before, after = ends
    there = swap(jnp.stack(put(before, after, lax.axis_index("xh") == 0, own)), xh=across)
    return before + there[0], after + own + there[1]


def shards(corr, slope_prev, kappa, detuning, pump, rho):
    small = (v.reshape(64, 128) for v in (kappa, detuning, pump))
    held = (pltpu.with_memory_space_constraint(v, pltpu.HBM) for v in (corr, slope_prev, *small))
    sec, own_rows, own_cols, kap_rows, kappa, detune, pump = sums(*held)
    tie = lax.optimization_barrier
    z = lax.axis_index("z")
    quad, row = row_quad(own_rows)
    pair, col = col_pair(own_cols)
    quad, pair = tie((quad, pair))
    got, row = row_step(quad, row, across, z % 2 == 1)
    col = col_line(pair, col)
    two, sec, col = tie((quad + got, sec, col))
    four, row = row_step(two, row, z_next, (z % 2 == 0) & (z != 0) | (z == 7))
    base, rhos = rows_part(rho, sec, kap_rows, kappa, detune, pump)
    col_b, col_a = col_ends(own_cols, col)
    four, base = tie((four, base))
    row_b, row_a = row_ends(two, four, row)
    base = cols_part(rho, sec, kappa, base)
    col_d = lines(rhos, col_b, col_a)
    return last(rhos, kappa, kap_rows, base, row_b, row_a, col_d)


def solution(mesh):
    fine = Mesh(mesh.devices.reshape(SIZES), AXES)
    placed = P(None, ROW, COL)
    return jax.shard_map(
        shards,
        mesh=fine,
        in_specs=(placed, placed, P(), P(), P(), P()),
        out_specs=placed,
        check_vma=False,
    )
```

```python
import itertools

import jax
import jax.numpy as jnp
from jax import lax
from jax.experimental import pallas as pl
from jax.experimental.pallas import tpu as pltpu
from jax.sharding import Mesh, PartitionSpec as P

AXES = ("xl", "z", "core", "y", "xh")
SIZES = (2, 8, 2, 4, 2)
ROW = AXES[:3]
COL = AXES[3:]
PLACES = [dict(zip(AXES, place)) for place in itertools.product(*map(range, SIZES))]


LANES = 128
BLOCK = 256
MIB = 1 << 20


def flat(place):
    index = 0
    for axis, size in zip(AXES, SIZES):
        index = index * size + place[axis]
    return index


def exchange(x, role1, role0):
    pairs = []
    for p in PLACES:
        partners = (role0, role1)[p["core"]]
        if partners:
            there = {axis: partner(p[axis]) for axis, partner in partners.items()}
            pairs.append((flat(p), flat({**p, **there})))
    return lax.ppermute(x, AXES, pairs)


def across(i):
    return i ^ 1


def z_next(z):
    return (z + 1) % 8 if z % 2 else (z - 1) % 8


def z_far(z):
    return (3, 6, 5, 0, 7, 2, 1, 4)[z]


def y_next(y):
    return (y + 1) % 4 if y % 2 else (y - 1) % 4


def spot():
    row = (lax.axis_index("xl") * 8 + lax.axis_index("z")) * 2 + lax.axis_index("core")
    col = lax.axis_index("y") * 2 + lax.axis_index("xh")
    return row, col


def sides():
    xl, z, core, y, xh = (lax.axis_index(axis) for axis in AXES)
    odd = core == 1
    next_z = ((z % 2 == 0) & (z != 0)) | (z == 7)
    return (
        odd,
        jnp.where(odd, z, y) % 2 == 1,
        (odd & next_z) | (~odd & (y >= 2)),
        (z <= 2) | (z == 4),
        (z == 1) | (z == 2) | (z == 4) | (z == 7),
        xh == 0,
        xl == 1,
    )


def down_rows(ref, row):
    halves = []
    for half in range(2):
        lanes = ref[pl.ds(row * 2 + half, 1), :]
        halves.append(jnp.broadcast_to(lanes, (LANES, LANES)).T)
    return jnp.concatenate(halves, axis=0)


EDGES = (0, 64, 128, 192, 224, 256)


def sums_kernel(
    corr_hbm, slope_hbm, kappa_hbm, detune_hbm, pump_hbm,
    sec_ref, sums_ref, kap_rows, kappa_buf, detune_ref, pump_ref, sides_ref,
    corr_buf, slope_buf, col_part, sems, small_sems,
):
    row, col = spot()
    core = lax.axis_index("core")
    kappa_copy, *late = [
        pltpu.make_async_copy(there, here, small_sems.at[n])
        for n, (there, here) in enumerate(
            ((kappa_hbm, kappa_buf), (detune_hbm, detune_ref), (pump_hbm, pump_ref))
        )
    ]
    kappa_copy.start()
    copies = []
    for c, (lo, hi) in enumerate(zip(EDGES, EDGES[1:])):
        part = pl.ds(lo, hi - lo)
        pair = (
            pltpu.make_async_copy(corr_hbm.at[:, part], corr_buf.at[:, part], sems.at[0, c]),
            pltpu.make_async_copy(slope_hbm.at[:, part], slope_buf.at[:, part], sems.at[1, c]),
        )
        for copy in pair:
            copy.start()
        copies.append(pair)
    for copy in late:
        copy.start()
    for n, side in enumerate(sides()):
        sides_ref[n] = jnp.full((2, 1024), jnp.where(side, 1.0, 0.0))
    kappa_copy.wait()
    kap_rows[...] = down_rows(kappa_buf, row)
    kap_cols = [
        jnp.broadcast_to(kappa_buf[pl.ds(col * 8 + b, 1), :], (8, LANES)) for b in range(8)
    ]
    totals = tuple(jnp.zeros((8, LANES), jnp.float32) for _ in range(16))
    for c, (lo, hi) in enumerate(zip(EDGES, EDGES[1:])):
        for copy in copies[c]:
            copy.wait()

        def group(g, totals):
            totals = list(totals)
            at = pl.ds(pl.multiple_of(lo + g * 8, 8), 8)
            kr = kap_rows[at, :]
            for p in range(2):
                along = None
                for b in range(8):
                    lanes = pl.ds(b * LANES, LANES)
                    s = corr_buf[p, at, lanes] + 0.25 * slope_buf[p, at, lanes]
                    sec_ref[p, at, lanes] = s
                    totals[p * 8 + b] = totals[p * 8 + b] + s * kr
                    w = s * kap_cols[b]
                    along = w if along is None else along + w
                col_part[p, at, :] = along
            return tuple(totals)

        totals = lax.fori_loop(0, (hi - lo) // 8, group, totals, unroll=2)
    for p in range(2):
        for b in range(8):
            total = jnp.sum(totals[p * 8 + b], axis=0, keepdims=True)
            sums_ref[pl.ds(p, 1), pl.ds(b * LANES, LANES)] = total
        for half in range(2):
            along = jnp.sum(col_part[p, pl.ds(half * LANES, LANES), :].T, axis=0, keepdims=True)
            for c in range(2):
                sums_ref[pl.ds(p, 1), pl.ds(1024 + c * 256 + half * LANES, LANES)] = jnp.where(
                    core == c, along, 0.0
                )
    sums_ref[:, pl.ds(1536, 512)] = jnp.zeros((2, 512), jnp.float32)
    for copy in late:
        copy.wait()


def split(x):
    high = x.astype(jnp.bfloat16)
    return high, (x - high.astype(jnp.float32)).astype(jnp.bfloat16)


def table(lower):
    a = lax.broadcasted_iota(jnp.int32, (BLOCK, BLOCK), 0)
    b = lax.broadcasted_iota(jnp.int32, (BLOCK, BLOCK), 1)
    before = (b < a) if lower else (a < b)
    return jnp.where(before, 1.0, jnp.where(a == b, 0.5, 0.0)).astype(jnp.bfloat16)


def matmul(a, b):
    return jnp.dot(a, b, preferred_element_type=jnp.float32)


def twice(x):
    return jnp.concatenate([x, x], axis=1)


def along_lanes(ref, first):
    return jnp.concatenate([ref[pl.ds(first, 1), :], ref[pl.ds(first + 1, 1), :]], axis=1)


def rows_kernel(rho_ref, sec_ref, kap_rows, kappa_ref, detune_ref, pump_ref, base_ref, rho_out):
    row, col = spot()
    rho_re, rho_im = rho_ref[0], rho_ref[1]
    rho_out[0] = jnp.full((8, LANES), rho_re)
    rho_out[1] = jnp.full((8, LANES), rho_im)
    e, f = 1.0 - rho_re, -rho_im
    kr = twice(kap_rows[...])
    dr = twice(down_rows(detune_ref, row))
    pr = twice(down_rows(pump_ref, row))
    mre_r = (0.5 * rho_re) * kr * kr
    mim_r = (0.5 * rho_im) * kr * kr - dr
    lower = table(True)
    for b in range(1024 // BLOCK):
        lanes = pl.ds(b * BLOCK, BLOCK)
        kc = along_lanes(kappa_ref, col * 8 + 2 * b)
        dc = along_lanes(detune_ref, col * 8 + 2 * b)
        q = []
        for p in range(2):
            high, low = split(sec_ref[p, :, lanes] * kr)
            q.append(matmul(lower, high) + matmul(lower, low))
        s_re, s_im = sec_ref[0, :, lanes], sec_ref[1, :, lanes]
        m_re = mre_r + (0.5 * rho_re) * kc * kc
        m_im = mim_r + (dc - (0.5 * rho_im) * kc * kc)
        i = lax.broadcasted_iota(jnp.int32, (256, BLOCK), 0) + row * 256
        k = lax.broadcasted_iota(jnp.int32, (256, BLOCK), 1) + (col * 1024 + b * BLOCK)
        base_ref[0, :, lanes] = (
            m_re * s_re - m_im * s_im - kr * (e * q[0] - f * q[1]) + jnp.where(i == k, pr, 0.0)
        )
        base_ref[1, :, lanes] = m_re * s_im + m_im * s_re - kr * (e * q[1] + f * q[0])


def cols_kernel(rho_ref, sec_ref, kappa_ref, part_ref, base_ref):
    _, col = spot()
    e, f = 1.0 - rho_ref[0], rho_ref[1]
    upper = table(False)
    carry = [jnp.zeros((256, 1), jnp.float32) for _ in range(2)]
    for b in range(1024 // BLOCK):
        lanes = pl.ds(b * BLOCK, BLOCK)
        kc = along_lanes(kappa_ref, col * 8 + 2 * b)
        q = []
        for p in range(2):
            w = sec_ref[p, :, lanes] * kc
            high, low = split(w)
            q.append(matmul(high, upper) + matmul(low, upper) + carry[p])
            carry[p] = carry[p] + jnp.sum(w, axis=1, keepdims=True)
        base_ref[0, :, lanes] = part_ref[0, :, lanes] - kc * (e * q[0] - f * q[1])
        base_ref[1, :, lanes] = part_ref[1, :, lanes] - kc * (e * q[1] + f * q[0])


def carried(rho_ref, before, after, lanes, sign, height):
    rho_re, rho_im = rho_ref[0, 0:1, :], sign * rho_ref[1, 0:1, :]
    b, a = before[:, lanes], after[:, lanes]
    both = b[0:1] + (rho_re * a[0:1] - rho_im * a[1:2]), b[1:2] + (rho_re * a[1:2] + rho_im * a[0:1])
    return [jnp.broadcast_to(x, (height, LANES)) for x in both]


def lines_kernel(rho_ref, before, after, down_ref):
    for half in range(2):
        at = pl.ds(half * LANES, LANES)
        for p, x in enumerate(carried(rho_ref, before, after, at, -1.0, LANES)):
            down_ref[p, at, :] = x.T


OUT_EDGES = (0, 32, 64, 128, 192, 224, 256)


def last_kernel(
    rho_ref, kappa_ref, kap_rows, base_ref, before, after, col_d, out_hbm, out_buf, sems
):
    _, col = spot()
    kap_cols = [
        jnp.broadcast_to(kappa_ref[pl.ds(col * 8 + b, 1), :], (8, LANES)) for b in range(8)
    ]
    row_ds = [
        carried(rho_ref, before, after, pl.ds(b * LANES, LANES), 1.0, 8) for b in range(8)
    ]
    copies = []
    for c, (lo, hi) in enumerate(zip(OUT_EDGES, OUT_EDGES[1:])):

        def group(g, carry):
            at = pl.ds(pl.multiple_of(lo + g * 8, 8), 8)
            kr = kap_rows[at, :]
            for p in range(2):
                dc = col_d[p, at, :]
                for b in range(8):
                    lanes = pl.ds(b * LANES, LANES)
                    out_buf[p, at, lanes] = base_ref[p, at, lanes] - (
                        kr * row_ds[b][p] + kap_cols[b] * dc
                    )
            return carry

        lax.fori_loop(0, (hi - lo) // 8, group, 0, unroll=2)
        part = pl.ds(lo, hi - lo)
        copy = pltpu.make_async_copy(out_buf.at[:, part], out_hbm.at[:, part], sems.at[c])
        copy.start()
        copies.append(copy)
    for copy in copies:
        copy.wait()


VM = pl.BlockSpec(memory_space=pltpu.VMEM)
SM = pl.BlockSpec(memory_space=pltpu.SMEM)
HB = pl.BlockSpec(memory_space=pltpu.HBM)
F32 = jnp.float32


def call(kernel, outs, ins, out_specs, scratch=(), alias={}, flops=0, limit=20):
    return pl.pallas_call(
        kernel,
        out_shape=outs,
        in_specs=ins,
        out_specs=out_specs,
        scratch_shapes=list(scratch),
        input_output_aliases=alias,
        cost_estimate=pl.CostEstimate(flops=flops, bytes_accessed=6 * MIB, transcendentals=0),
        compiler_params=pltpu.CompilerParams(vmem_limit_bytes=limit * MIB),
    )


def vmem(*shape):
    return pltpu.VMEM(shape, F32)


WHOLE = (2, 256, 1024)
DMA = pltpu.SemaphoreType.DMA


def sums(corr, slope, *small):
    return call(
        sums_kernel,
        [vmem(*WHOLE), vmem(2, 2048), vmem(256, 128)] + [vmem(64, 128)] * 3 + [vmem(7, 2, 1024)],
        [HB] * 5,
        [VM] * 7,
        [vmem(*WHOLE), vmem(*WHOLE), vmem(2, 256, 128), DMA((2, len(EDGES) - 1)), DMA((3,))],
    )(corr, slope, *small)


def rows_part(rho, sec, kap_rows, *small):
    return call(
        rows_kernel, [vmem(*WHOLE), vmem(2, 8, 128)], [SM] + [VM] * 5, [VM] * 2, flops=10**9
    )(rho, sec, kap_rows, *small)


def cols_part(rho, sec, kappa, part):
    return call(cols_kernel, vmem(*WHOLE), [SM] + [VM] * 3, VM, alias={3: 0}, flops=10**9)(
        rho, sec, kappa, part
    )


def lines(rho, before, after):
    return call(lines_kernel, vmem(2, 256, 128), [VM] * 3, VM, limit=4)(rho, before, after)


def last(*operands):
    return call(
        last_kernel,
        jax.ShapeDtypeStruct(WHOLE, F32),
        [VM] * 7,
        HB,
        [vmem(*WHOLE), DMA((len(OUT_EDGES) - 1,))],
    )(*operands)


def put(before, after, lower, x):
    return before + jnp.where(lower, x, 0.0), after + jnp.where(lower, 0.0, x)


def shards(corr, slope_prev, kappa, detuning, pump, rho):
    small = (v.reshape(64, 128) for v in (kappa, detuning, pump))
    held = (pltpu.with_memory_space_constraint(v, pltpu.HBM) for v in (corr, slope_prev, *small))
    sec, own, kap_rows, kappa, detune, pump, places = sums(*held)
    odd, lower1, lower2, far1, far2, xh_first, xl_last = (place > 0.5 for place in places)
    tie = lax.optimization_barrier
    other_core = {"core": across}

    theirs = exchange(own, other_core, other_core)
    chip = own + theirs
    mine = jnp.where(odd, chip[:, :1024], chip[:, 1024:])
    mine, sec = tie((mine, sec))
    got = exchange(mine, {"z": across}, {"y": across})
    base, rhos = rows_part(rho, sec, kap_rows, kappa, detune, pump)
    zero = jnp.zeros_like(mine)
    before, after = put(zero, zero, lower1, got)
    pair = mine + got
    pair, base = tie((pair, base))
    got = exchange(pair, {"z": z_next}, {"y": y_next})
    base = cols_part(rho, sec, kappa, base)
    got, base = tie((got, base))
    before, after = put(before, after, lower2, got)
    far = put(zero, zero, far1, pair)
    far = put(*far, far2, got)
    near = put(before, after, xh_first, mine)
    there = jnp.stack([jnp.where(odd, f, n) for f, n in zip(far, near)])
    got = exchange(there, {"z": z_far}, {"xh": across})
    before, after = before + got[0], after + got[1]
    got = exchange(mine + before + after, {"xl": across}, None)
    before, after = put(before, after, xl_last, got)
    got = exchange(jnp.stack([before, after]), other_core, other_core)
    rows = [jnp.where(odd, here, there) for here, there in zip((before, after), got)]
    rows = put(*rows, odd, theirs[:, :1024])
    cols = [
        jnp.where(odd[:, :256], there[:, 256:512], here[:, :256])
        for here, there in zip((before, after), got)
    ]
    own_cols = jnp.where(odd[:, :256], own[:, 1280:1536], own[:, 1024:1280])
    col_d = lines(rhos, cols[0], cols[1] + own_cols)
    return last(rhos, kappa, kap_rows, base, rows[0], rows[1] + own[:, :1024], col_d)


def solution(mesh):
    fine = Mesh(mesh.devices.reshape(SIZES), AXES)
    placed = P(None, ROW, COL)
    return jax.shard_map(
        shards,
        mesh=fine,
        in_specs=(placed, placed, P(), P(), P(), P()),
        out_specs=placed,
        check_vma=False,
    )
```

```python
import itertools

import jax
import jax.numpy as jnp
from jax import lax
from jax.experimental import pallas as pl
from jax.experimental.pallas import tpu as pltpu
from jax.sharding import Mesh, PartitionSpec as P

AXES = ("xl", "z", "core", "y", "xh")
SIZES = (2, 8, 2, 4, 2)
ROW = AXES[:3]
COL = AXES[3:]
PLACES = [dict(zip(AXES, place)) for place in itertools.product(*map(range, SIZES))]


LANES = 128
BLOCK = 256
MIB = 1 << 20


def flat(place):
    index = 0
    for axis, size in zip(AXES, SIZES):
        index = index * size + place[axis]
    return index


def exchange(x, role1, role0):
    pairs = []
    for p in PLACES:
        partners = (role0, role1)[p["core"]]
        if partners:
            there = {axis: partner(p[axis]) for axis, partner in partners.items()}
            pairs.append((flat(p), flat({**p, **there})))
    return lax.ppermute(x, AXES, pairs)


def across(i):
    return i ^ 1


def z_next(z):
    return (z + 1) % 8 if z % 2 else (z - 1) % 8


def z_far(z):
    return (3, 6, 5, 0, 7, 2, 1, 4)[z]


def y_next(y):
    return (y + 1) % 4 if y % 2 else (y - 1) % 4


def spot():
    row = (lax.axis_index("xl") * 8 + lax.axis_index("z")) * 2 + lax.axis_index("core")
    col = lax.axis_index("y") * 2 + lax.axis_index("xh")
    return row, col


def sides():
    xl, z, core, y, xh = (lax.axis_index(axis) for axis in AXES)
    odd = core == 1
    next_z = ((z % 2 == 0) & (z != 0)) | (z == 7)
    return (
        odd,
        jnp.where(odd, z, y) % 2 == 1,
        (odd & next_z) | (~odd & (y >= 2)),
        (z <= 2) | (z == 4),
        (z == 1) | (z == 2) | (z == 4) | (z == 7),
        xh == 0,
        xl == 1,
    )


def down_rows(ref, row):
    halves = []
    for half in range(2):
        lanes = ref[pl.ds(row * 2 + half, 1), :]
        halves.append(jnp.broadcast_to(lanes, (LANES, LANES)).T)
    return jnp.concatenate(halves, axis=0)


EDGES = (0, 64, 128, 192, 240, 256)


def sums_kernel(
    corr_hbm, slope_hbm, kappa_hbm, detune_hbm, pump_hbm,
    sec_ref, sums_ref, kap_rows, kappa_buf, detune_ref, pump_ref, sides_ref,
    corr_buf, slope_buf, col_part, sems, small_sems,
):
    row, col = spot()
    core = lax.axis_index("core")
    kappa_copy, *late = [
        pltpu.make_async_copy(there, here, small_sems.at[n])
        for n, (there, here) in enumerate(
            ((kappa_hbm, kappa_buf), (detune_hbm, detune_ref), (pump_hbm, pump_ref))
        )
    ]
    kappa_copy.start()
    copies = []
    for c, (lo, hi) in enumerate(zip(EDGES, EDGES[1:])):
        part = pl.ds(lo, hi - lo)
        pair = (
            pltpu.make_async_copy(corr_hbm.at[:, part], corr_buf.at[:, part], sems.at[0, c]),
            pltpu.make_async_copy(slope_hbm.at[:, part], slope_buf.at[:, part], sems.at[1, c]),
        )
        for copy in pair:
            copy.start()
        copies.append(pair)
    for copy in late:
        copy.start()
    sums_ref[:, pl.ds(1536, 512)] = jnp.zeros((2, 512), jnp.float32)
    for n, side in enumerate(sides()):
        sides_ref[n] = jnp.full((2, 1024), jnp.where(side, 1.0, 0.0))
    kappa_copy.wait()
    kap_rows[...] = down_rows(kappa_buf, row)
    kap_cols = [
        jnp.broadcast_to(kappa_buf[pl.ds(col * 8 + b, 1), :], (8, LANES)) for b in range(8)
    ]
    totals = tuple(jnp.zeros((8, LANES), jnp.float32) for _ in range(16))
    for c, (lo, hi) in enumerate(zip(EDGES, EDGES[1:])):
        for copy in copies[c]:
            copy.wait()

        def group(g, totals):
            totals = list(totals)
            at = pl.ds(pl.multiple_of(lo + g * 8, 8), 8)
            kr = kap_rows[at, :]
            for p in range(2):
                along = None
                for b in range(8):
                    lanes = pl.ds(b * LANES, LANES)
                    s = corr_buf[p, at, lanes] + 0.25 * slope_buf[p, at, lanes]
                    sec_ref[p, at, lanes] = s
                    totals[p * 8 + b] = totals[p * 8 + b] + s * kr
                    w = s * kap_cols[b]
                    along = w if along is None else along + w
                col_part[p, at, :] = along
            return tuple(totals)

        totals = lax.fori_loop(0, (hi - lo) // 8, group, totals, unroll=2)
        if hi % LANES == 0:
            half = pl.ds(hi - LANES, LANES)
            for p in range(2):
                along = jnp.sum(col_part[p, half, :].T, axis=0, keepdims=True)
                for c in range(2):
                    sums_ref[pl.ds(p, 1), pl.ds(1024 + c * 256 + hi - LANES, LANES)] = jnp.where(
                        core == c, along, 0.0
                    )
    for p in range(2):
        for b in range(8):
            total = jnp.sum(totals[p * 8 + b], axis=0, keepdims=True)
            sums_ref[pl.ds(p, 1), pl.ds(b * LANES, LANES)] = total
    for copy in late:
        copy.wait()


def split(x):
    high = x.astype(jnp.bfloat16)
    return high, (x - high.astype(jnp.float32)).astype(jnp.bfloat16)


def table(lower):
    a = lax.broadcasted_iota(jnp.int32, (BLOCK, BLOCK), 0)
    b = lax.broadcasted_iota(jnp.int32, (BLOCK, BLOCK), 1)
    before = (b < a) if lower else (a < b)
    return jnp.where(before, 1.0, jnp.where(a == b, 0.5, 0.0)).astype(jnp.bfloat16)


def matmul(a, b):
    return jnp.dot(a, b, preferred_element_type=jnp.float32)


def twice(x):
    return jnp.concatenate([x, x], axis=1)


def along_lanes(ref, first):
    return jnp.concatenate([ref[pl.ds(first, 1), :], ref[pl.ds(first + 1, 1), :]], axis=1)


def rows_kernel(rho_ref, sec_ref, kap_rows, kappa_ref, detune_ref, pump_ref, base_ref, rho_out):
    row, col = spot()
    rho_re, rho_im = rho_ref[0], rho_ref[1]
    rho_out[0] = jnp.full((8, LANES), rho_re)
    rho_out[1] = jnp.full((8, LANES), rho_im)
    e, f = 1.0 - rho_re, -rho_im
    kr = twice(kap_rows[...])
    dr = twice(down_rows(detune_ref, row))
    pr = twice(down_rows(pump_ref, row))
    mre_r = (0.5 * rho_re) * kr * kr
    mim_r = (0.5 * rho_im) * kr * kr - dr
    lower = table(True)
    for b in range(1024 // BLOCK):
        lanes = pl.ds(b * BLOCK, BLOCK)
        kc = along_lanes(kappa_ref, col * 8 + 2 * b)
        dc = along_lanes(detune_ref, col * 8 + 2 * b)
        q = []
        for p in range(2):
            high, low = split(sec_ref[p, :, lanes] * kr)
            q.append(matmul(lower, high) + matmul(lower, low))
        s_re, s_im = sec_ref[0, :, lanes], sec_ref[1, :, lanes]
        m_re = mre_r + (0.5 * rho_re) * kc * kc
        m_im = mim_r + (dc - (0.5 * rho_im) * kc * kc)
        i = lax.broadcasted_iota(jnp.int32, (256, BLOCK), 0) + row * 256
        k = lax.broadcasted_iota(jnp.int32, (256, BLOCK), 1) + (col * 1024 + b * BLOCK)
        base_ref[0, :, lanes] = (
            m_re * s_re - m_im * s_im - kr * (e * q[0] - f * q[1]) + jnp.where(i == k, pr, 0.0)
        )
        base_ref[1, :, lanes] = m_re * s_im + m_im * s_re - kr * (e * q[1] + f * q[0])


def cols_kernel(rho_ref, sec_ref, kappa_ref, part_ref, base_ref):
    _, col = spot()
    e, f = 1.0 - rho_ref[0], rho_ref[1]
    upper = table(False)
    carry = [jnp.zeros((256, 1), jnp.float32) for _ in range(2)]
    for b in range(1024 // BLOCK):
        lanes = pl.ds(b * BLOCK, BLOCK)
        kc = along_lanes(kappa_ref, col * 8 + 2 * b)
        q = []
        for p in range(2):
            w = sec_ref[p, :, lanes] * kc
            high, low = split(w)
            q.append(matmul(high, upper) + matmul(low, upper) + carry[p])
            carry[p] = carry[p] + jnp.sum(w, axis=1, keepdims=True)
        base_ref[0, :, lanes] = part_ref[0, :, lanes] - kc * (e * q[0] - f * q[1])
        base_ref[1, :, lanes] = part_ref[1, :, lanes] - kc * (e * q[1] + f * q[0])


def carried(rho_ref, before, after, lanes, sign, height):
    rho_re, rho_im = rho_ref[0, 0:1, :], sign * rho_ref[1, 0:1, :]
    b, a = before[:, lanes], after[:, lanes]
    both = b[0:1] + (rho_re * a[0:1] - rho_im * a[1:2]), b[1:2] + (rho_re * a[1:2] + rho_im * a[0:1])
    return [jnp.broadcast_to(x, (height, LANES)) for x in both]


def lines_kernel(rho_ref, before, after, down_ref):
    for half in range(2):
        at = pl.ds(half * LANES, LANES)
        for p, x in enumerate(carried(rho_ref, before, after, at, -1.0, LANES)):
            down_ref[p, at, :] = x.T


OUT_EDGES = (0, 32, 64, 128, 192, 224, 256)


def last_kernel(
    rho_ref, kappa_ref, kap_rows, base_ref, before, after, col_d, out_hbm, out_buf, sems
):
    _, col = spot()
    kap_cols = [
        jnp.broadcast_to(kappa_ref[pl.ds(col * 8 + b, 1), :], (8, LANES)) for b in range(8)
    ]
    row_ds = [
        carried(rho_ref, before, after, pl.ds(b * LANES, LANES), 1.0, 8) for b in range(8)
    ]
    copies = []
    for c, (lo, hi) in enumerate(zip(OUT_EDGES, OUT_EDGES[1:])):

        def group(g, carry):
            at = pl.ds(pl.multiple_of(lo + g * 8, 8), 8)
            kr = kap_rows[at, :]
            for p in range(2):
                dc = col_d[p, at, :]
                for b in range(8):
                    lanes = pl.ds(b * LANES, LANES)
                    out_buf[p, at, lanes] = base_ref[p, at, lanes] - (
                        kr * row_ds[b][p] + kap_cols[b] * dc
                    )
            return carry

        lax.fori_loop(0, (hi - lo) // 8, group, 0, unroll=2)
        part = pl.ds(lo, hi - lo)
        copy = pltpu.make_async_copy(out_buf.at[:, part], out_hbm.at[:, part], sems.at[c])
        copy.start()
        copies.append(copy)
    for copy in copies:
        copy.wait()


VM = pl.BlockSpec(memory_space=pltpu.VMEM)
SM = pl.BlockSpec(memory_space=pltpu.SMEM)
HB = pl.BlockSpec(memory_space=pltpu.HBM)
F32 = jnp.float32


def call(kernel, outs, ins, out_specs, scratch=(), alias={}, flops=0, limit=20):
    return pl.pallas_call(
        kernel,
        out_shape=outs,
        in_specs=ins,
        out_specs=out_specs,
        scratch_shapes=list(scratch),
        input_output_aliases=alias,
        cost_estimate=pl.CostEstimate(flops=flops, bytes_accessed=6 * MIB, transcendentals=0),
        compiler_params=pltpu.CompilerParams(vmem_limit_bytes=limit * MIB),
    )


def vmem(*shape):
    return pltpu.VMEM(shape, F32)


WHOLE = (2, 256, 1024)
DMA = pltpu.SemaphoreType.DMA


def sums(corr, slope, *small):
    return call(
        sums_kernel,
        [vmem(*WHOLE), vmem(2, 2048), vmem(256, 128)] + [vmem(64, 128)] * 3 + [vmem(7, 2, 1024)],
        [HB] * 5,
        [VM] * 7,
        [vmem(*WHOLE), vmem(*WHOLE), vmem(2, 256, 128), DMA((2, len(EDGES) - 1)), DMA((3,))],
    )(corr, slope, *small)


def rows_part(rho, sec, kap_rows, *small):
    return call(
        rows_kernel, [vmem(*WHOLE), vmem(2, 8, 128)], [SM] + [VM] * 5, [VM] * 2, flops=10**9
    )(rho, sec, kap_rows, *small)


def cols_part(rho, sec, kappa, part):
    return call(cols_kernel, vmem(*WHOLE), [SM] + [VM] * 3, VM, alias={3: 0}, flops=10**9)(
        rho, sec, kappa, part
    )


def lines(rho, before, after):
    return call(lines_kernel, vmem(2, 256, 128), [VM] * 3, VM, limit=4)(rho, before, after)


def last(*operands):
    return call(
        last_kernel,
        jax.ShapeDtypeStruct(WHOLE, F32),
        [VM] * 7,
        HB,
        [vmem(*WHOLE), DMA((len(OUT_EDGES) - 1,))],
    )(*operands)


def put(before, after, lower, x):
    return before + jnp.where(lower, x, 0.0), after + jnp.where(lower, 0.0, x)


def shards(corr, slope_prev, kappa, detuning, pump, rho):
    small = (v.reshape(64, 128) for v in (kappa, detuning, pump))
    held = (pltpu.with_memory_space_constraint(v, pltpu.HBM) for v in (corr, slope_prev, *small))
    sec, own, kap_rows, kappa, detune, pump, places = sums(*held)
    odd, lower1, lower2, far1, far2, xh_first, xl_last = (place > 0.5 for place in places)
    tie = lax.optimization_barrier
    other_core = {"core": across}

    theirs = exchange(own, other_core, other_core)
    chip = own + theirs
    mine = jnp.where(odd, chip[:, :1024], chip[:, 1024:])
    mine, sec = tie((mine, sec))
    got = exchange(mine, {"z": across}, {"y": across})
    base, rhos = rows_part(rho, sec, kap_rows, kappa, detune, pump)
    zero = jnp.zeros_like(mine)
    before, after = put(zero, zero, lower1, got)
    pair = mine + got
    pair, base = tie((pair, base))
    got = exchange(pair, {"z": z_next}, {"y": y_next})
    got, base = tie((got, base))
    base = cols_part(rho, sec, kappa, base)
    before, after = put(before, after, lower2, got)
    far = put(zero, zero, far1, pair)
    far = put(*far, far2, got)
    near = put(before, after, xh_first, mine)
    there = jnp.stack([jnp.where(odd, f, n) for f, n in zip(far, near)])
    got = exchange(there, {"z": z_far}, {"xh": across})
    before, after = before + got[0], after + got[1]
    line, base = tie((mine + before + after, base))
    got = exchange(line, {"xl": across}, None)
    before, after = put(before, after, xl_last, got)
    got = exchange(jnp.stack([before, after]), other_core, other_core)
    rows = [jnp.where(odd, here, there) for here, there in zip((before, after), got)]
    rows = put(*rows, odd, theirs[:, :1024])
    cols = [
        jnp.where(odd[:, :256], there[:, 256:512], here[:, :256])
        for here, there in zip((before, after), got)
    ]
    own_cols = jnp.where(odd[:, :256], own[:, 1280:1536], own[:, 1024:1280])
    col_d = lines(rhos, cols[0], cols[1] + own_cols)
    return last(rhos, kappa, kap_rows, base, rows[0], rows[1] + own[:, :1024], col_d)


def solution(mesh):
    fine = Mesh(mesh.devices.reshape(SIZES), AXES)
    placed = P(None, ROW, COL)
    return jax.shard_map(
        shards,
        mesh=fine,
        in_specs=(placed, placed, P(), P(), P(), P()),
        out_specs=placed,
        check_vma=False,
    )
```

```python
import itertools

import jax
import jax.numpy as jnp
from jax import lax
from jax.experimental import pallas as pl
from jax.experimental.pallas import tpu as pltpu
from jax.sharding import Mesh, PartitionSpec as P

AXES = ("xl", "z", "core", "y", "xh")
SIZES = (2, 8, 2, 4, 2)
ROW = AXES[:3]
COL = AXES[3:]
PLACES = [dict(zip(AXES, place)) for place in itertools.product(*map(range, SIZES))]


LANES = 128
BLOCK = 256
MIB = 1 << 20


def flat(place):
    index = 0
    for axis, size in zip(AXES, SIZES):
        index = index * size + place[axis]
    return index


def exchange(x, role1, role0):
    pairs = []
    for p in PLACES:
        partners = (role0, role1)[p["core"]]
        if partners:
            there = {axis: partner(p[axis]) for axis, partner in partners.items()}
            pairs.append((flat(p), flat({**p, **there})))
    return lax.ppermute(x, AXES, pairs)


def across(i):
    return i ^ 1


def z_next(z):
    return (z + 1) % 8 if z % 2 else (z - 1) % 8


def z_far(z):
    return (3, 6, 5, 0, 7, 2, 1, 4)[z]


def y_next(y):
    return (y + 1) % 4 if y % 2 else (y - 1) % 4


def spot():
    row = (lax.axis_index("xl") * 8 + lax.axis_index("z")) * 2 + lax.axis_index("core")
    col = lax.axis_index("y") * 2 + lax.axis_index("xh")
    return row, col


def sides():
    xl, z, core, y, xh = (lax.axis_index(axis) for axis in AXES)
    odd = core == 1
    next_z = ((z % 2 == 0) & (z != 0)) | (z == 7)
    return (
        odd,
        jnp.where(odd, z, y) % 2 == 1,
        (odd & next_z) | (~odd & (y >= 2)),
        (z <= 2) | (z == 4),
        (z == 1) | (z == 2) | (z == 4) | (z == 7),
        xh == 0,
        xl == 1,
    )


def down_rows(ref, row):
    halves = []
    for half in range(2):
        lanes = ref[pl.ds(row * 2 + half, 1), :]
        halves.append(jnp.broadcast_to(lanes, (LANES, LANES)).T)
    return jnp.concatenate(halves, axis=0)


PIECE = 32


def sums_kernel(
    corr_hbm, slope_hbm, kappa_hbm, detune_hbm, pump_hbm,
    sec_ref, sums_ref, kap_rows, kappa_buf, detune_ref, pump_ref, sides_ref,
    corr_buf, slope_buf, col_part, sems, small_sems,
):
    row, col = spot()
    core = lax.axis_index("core")
    kappa_copy, *late = [
        pltpu.make_async_copy(there, here, small_sems.at[n])
        for n, (there, here) in enumerate(
            ((kappa_hbm, kappa_buf), (detune_hbm, detune_ref), (pump_hbm, pump_ref))
        )
    ]
    kappa_copy.start()

    def piece(c):
        part = pl.ds(pl.multiple_of(c * PIECE, PIECE), PIECE)
        return (
            pltpu.make_async_copy(corr_hbm.at[:, part], corr_buf.at[:, part], sems.at[0, c]),
            pltpu.make_async_copy(slope_hbm.at[:, part], slope_buf.at[:, part], sems.at[1, c]),
        )

    @pl.loop(0, 256 // PIECE)
    def _(c):
        for copy in piece(c):
            copy.start()

    for copy in late:
        copy.start()
    sums_ref[:, pl.ds(1536, 512)] = jnp.zeros((2, 512), jnp.float32)
    for n, side in enumerate(sides()):
        sides_ref[n] = jnp.full((2, 1024), jnp.where(side, 1.0, 0.0))
    kappa_copy.wait()
    kap_rows[...] = down_rows(kappa_buf, row)
    kap_cols = [
        jnp.broadcast_to(kappa_buf[pl.ds(col * 8 + b, 1), :], (8, LANES)) for b in range(8)
    ]
    totals = tuple(jnp.zeros((8, LANES), jnp.float32) for _ in range(16))
    for c in range(256 // PIECE):
        lo, hi = c * PIECE, (c + 1) * PIECE
        for copy in piece(c):
            copy.wait()

        def group(g, totals):
            totals = list(totals)
            at = pl.ds(pl.multiple_of(lo + g * 8, 8), 8)
            kr = kap_rows[at, :]
            for p in range(2):
                along = None
                for b in range(8):
                    lanes = pl.ds(b * LANES, LANES)
                    s = corr_buf[p, at, lanes] + 0.25 * slope_buf[p, at, lanes]
                    sec_ref[p, at, lanes] = s
                    totals[p * 8 + b] = totals[p * 8 + b] + s * kr
                    w = s * kap_cols[b]
                    along = w if along is None else along + w
                col_part[p, at, :] = along
            return tuple(totals)

        totals = lax.fori_loop(0, (hi - lo) // 8, group, totals, unroll=2)
        if hi % LANES == 0:
            half = pl.ds(hi - LANES, LANES)
            for p in range(2):
                along = jnp.sum(col_part[p, half, :].T, axis=0, keepdims=True)
                for c in range(2):
                    sums_ref[pl.ds(p, 1), pl.ds(1024 + c * 256 + hi - LANES, LANES)] = jnp.where(
                        core == c, along, 0.0
                    )
    for p in range(2):
        for b in range(8):
            total = jnp.sum(totals[p * 8 + b], axis=0, keepdims=True)
            sums_ref[pl.ds(p, 1), pl.ds(b * LANES, LANES)] = total
    for copy in late:
        copy.wait()


def split(x):
    high = x.astype(jnp.bfloat16)
    return high, (x - high.astype(jnp.float32)).astype(jnp.bfloat16)


def table(lower):
    a = lax.broadcasted_iota(jnp.int32, (BLOCK, BLOCK), 0)
    b = lax.broadcasted_iota(jnp.int32, (BLOCK, BLOCK), 1)
    before = (b < a) if lower else (a < b)
    return jnp.where(before, 1.0, jnp.where(a == b, 0.5, 0.0)).astype(jnp.bfloat16)


def matmul(a, b):
    return jnp.dot(a, b, preferred_element_type=jnp.float32)


def twice(x):
    return jnp.concatenate([x, x], axis=1)


def along_lanes(ref, first):
    return jnp.concatenate([ref[pl.ds(first, 1), :], ref[pl.ds(first + 1, 1), :]], axis=1)


def rows_kernel(rho_ref, sec_ref, kap_rows, kappa_ref, detune_ref, pump_ref, base_ref, rho_out):
    row, col = spot()
    rho_re, rho_im = rho_ref[0], rho_ref[1]
    rho_out[0] = jnp.full((8, LANES), rho_re)
    rho_out[1] = jnp.full((8, LANES), rho_im)
    e, f = 1.0 - rho_re, -rho_im
    kr = twice(kap_rows[...])
    dr = twice(down_rows(detune_ref, row))
    pr = twice(down_rows(pump_ref, row))
    mre_r = (0.5 * rho_re) * kr * kr
    mim_r = (0.5 * rho_im) * kr * kr - dr
    lower = table(True)
    for b in range(1024 // BLOCK):
        lanes = pl.ds(b * BLOCK, BLOCK)
        kc = along_lanes(kappa_ref, col * 8 + 2 * b)
        dc = along_lanes(detune_ref, col * 8 + 2 * b)
        q = []
        for p in range(2):
            high, low = split(sec_ref[p, :, lanes] * kr)
            q.append(matmul(lower, high) + matmul(lower, low))
        s_re, s_im = sec_ref[0, :, lanes], sec_ref[1, :, lanes]
        m_re = mre_r + (0.5 * rho_re) * kc * kc
        m_im = mim_r + (dc - (0.5 * rho_im) * kc * kc)
        i = lax.broadcasted_iota(jnp.int32, (256, BLOCK), 0) + row * 256
        k = lax.broadcasted_iota(jnp.int32, (256, BLOCK), 1) + (col * 1024 + b * BLOCK)
        base_ref[0, :, lanes] = (
            m_re * s_re - m_im * s_im - kr * (e * q[0] - f * q[1]) + jnp.where(i == k, pr, 0.0)
        )
        base_ref[1, :, lanes] = m_re * s_im + m_im * s_re - kr * (e * q[1] + f * q[0])


def cols_kernel(rho_ref, sec_ref, kappa_ref, part_ref, base_ref):
    _, col = spot()
    e, f = 1.0 - rho_ref[0], rho_ref[1]
    upper = table(False)
    carry = [jnp.zeros((256, 1), jnp.float32) for _ in range(2)]
    for b in range(1024 // BLOCK):
        lanes = pl.ds(b * BLOCK, BLOCK)
        kc = along_lanes(kappa_ref, col * 8 + 2 * b)
        q = []
        for p in range(2):
            w = sec_ref[p, :, lanes] * kc
            high, low = split(w)
            q.append(matmul(high, upper) + matmul(low, upper) + carry[p])
            carry[p] = carry[p] + jnp.sum(w, axis=1, keepdims=True)
        base_ref[0, :, lanes] = part_ref[0, :, lanes] - kc * (e * q[0] - f * q[1])
        base_ref[1, :, lanes] = part_ref[1, :, lanes] - kc * (e * q[1] + f * q[0])


def carried(rho_ref, before, after, lanes, sign, height):
    rho_re, rho_im = rho_ref[0, 0:1, :], sign * rho_ref[1, 0:1, :]
    b, a = before[:, lanes], after[:, lanes]
    both = b[0:1] + (rho_re * a[0:1] - rho_im * a[1:2]), b[1:2] + (rho_re * a[1:2] + rho_im * a[0:1])
    return [jnp.broadcast_to(x, (height, LANES)) for x in both]


def lines_kernel(rho_ref, before, after, down_ref):
    for half in range(2):
        at = pl.ds(half * LANES, LANES)
        for p, x in enumerate(carried(rho_ref, before, after, at, -1.0, LANES)):
            down_ref[p, at, :] = x.T


OUT_EDGES = (0, 32, 64, 128, 192, 224, 256)


def last_kernel(
    rho_ref, kappa_ref, kap_rows, base_ref, before, after, col_d, out_hbm, out_buf, sems
):
    _, col = spot()
    kap_cols = [
        jnp.broadcast_to(kappa_ref[pl.ds(col * 8 + b, 1), :], (8, LANES)) for b in range(8)
    ]
    row_ds = [
        carried(rho_ref, before, after, pl.ds(b * LANES, LANES), 1.0, 8) for b in range(8)
    ]
    copies = []
    for c, (lo, hi) in enumerate(zip(OUT_EDGES, OUT_EDGES[1:])):

        def group(g, carry):
            at = pl.ds(pl.multiple_of(lo + g * 8, 8), 8)
            kr = kap_rows[at, :]
            for p in range(2):
                dc = col_d[p, at, :]
                for b in range(8):
                    lanes = pl.ds(b * LANES, LANES)
                    out_buf[p, at, lanes] = base_ref[p, at, lanes] - (
                        kr * row_ds[b][p] + kap_cols[b] * dc
                    )
            return carry

        lax.fori_loop(0, (hi - lo) // 8, group, 0, unroll=2)
        part = pl.ds(lo, hi - lo)
        copy = pltpu.make_async_copy(out_buf.at[:, part], out_hbm.at[:, part], sems.at[c])
        copy.start()
        copies.append(copy)
    for copy in copies:
        copy.wait()


VM = pl.BlockSpec(memory_space=pltpu.VMEM)
SM = pl.BlockSpec(memory_space=pltpu.SMEM)
HB = pl.BlockSpec(memory_space=pltpu.HBM)
F32 = jnp.float32


def call(kernel, outs, ins, out_specs, scratch=(), alias={}, flops=0, limit=20):
    return pl.pallas_call(
        kernel,
        out_shape=outs,
        in_specs=ins,
        out_specs=out_specs,
        scratch_shapes=list(scratch),
        input_output_aliases=alias,
        cost_estimate=pl.CostEstimate(flops=flops, bytes_accessed=6 * MIB, transcendentals=0),
        compiler_params=pltpu.CompilerParams(vmem_limit_bytes=limit * MIB),
    )


def vmem(*shape):
    return pltpu.VMEM(shape, F32)


WHOLE = (2, 256, 1024)
DMA = pltpu.SemaphoreType.DMA


def sums(corr, slope, *small):
    return call(
        sums_kernel,
        [vmem(*WHOLE), vmem(2, 2048), vmem(256, 128)] + [vmem(64, 128)] * 3 + [vmem(7, 2, 1024)],
        [HB] * 5,
        [VM] * 7,
        [vmem(*WHOLE), vmem(*WHOLE), vmem(2, 256, 128), DMA((2, 256 // PIECE)), DMA((3,))],
    )(corr, slope, *small)


def rows_part(rho, sec, kap_rows, *small):
    return call(
        rows_kernel, [vmem(*WHOLE), vmem(2, 8, 128)], [SM] + [VM] * 5, [VM] * 2, flops=10**9
    )(rho, sec, kap_rows, *small)


def cols_part(rho, sec, kappa, part):
    return call(cols_kernel, vmem(*WHOLE), [SM] + [VM] * 3, VM, alias={3: 0}, flops=10**9)(
        rho, sec, kappa, part
    )


def lines(rho, before, after):
    return call(lines_kernel, vmem(2, 256, 128), [VM] * 3, VM, limit=4)(rho, before, after)


def last(*operands):
    return call(
        last_kernel,
        jax.ShapeDtypeStruct(WHOLE, F32),
        [VM] * 7,
        HB,
        [vmem(*WHOLE), DMA((len(OUT_EDGES) - 1,))],
    )(*operands)


def put(before, after, lower, x):
    return before + jnp.where(lower, x, 0.0), after + jnp.where(lower, 0.0, x)


def shards(corr, slope_prev, kappa, detuning, pump, rho):
    small = (v.reshape(64, 128) for v in (kappa, detuning, pump))
    held = (pltpu.with_memory_space_constraint(v, pltpu.HBM) for v in (corr, slope_prev, *small))
    sec, own, kap_rows, kappa, detune, pump, places = sums(*held)
    odd, lower1, lower2, far1, far2, xh_first, xl_last = (place > 0.5 for place in places)
    tie = lax.optimization_barrier
    other_core = {"core": across}

    theirs = exchange(own, other_core, other_core)
    chip = own + theirs
    mine = jnp.where(odd, chip[:, :1024], chip[:, 1024:])
    mine, sec = tie((mine, sec))
    got = exchange(mine, {"z": across}, {"y": across})
    base, rhos = rows_part(rho, sec, kap_rows, kappa, detune, pump)
    zero = jnp.zeros_like(mine)
    before, after = put(zero, zero, lower1, got)
    pair = mine + got
    pair, base = tie((pair, base))
    got = exchange(pair, {"z": z_next}, {"y": y_next})
    got, base = tie((got, base))
    base = cols_part(rho, sec, kappa, base)
    before, after = put(before, after, lower2, got)
    far = put(zero, zero, far1, pair)
    far = put(*far, far2, got)
    near = put(before, after, xh_first, mine)
    there = jnp.stack([jnp.where(odd, f, n) for f, n in zip(far, near)])
    got = exchange(there, {"z": z_far}, {"xh": across})
    before, after = before + got[0], after + got[1]
    line, base = tie((mine + before + after, base))
    got = exchange(line, {"xl": across}, None)
    before, after = put(before, after, xl_last, got)
    got = exchange(jnp.stack([before, after]), other_core, other_core)
    rows = [jnp.where(odd, here, there) for here, there in zip((before, after), got)]
    rows = put(*rows, odd, theirs[:, :1024])
    cols = [
        jnp.where(odd[:, :256], there[:, 256:512], here[:, :256])
        for here, there in zip((before, after), got)
    ]
    own_cols = jnp.where(odd[:, :256], own[:, 1280:1536], own[:, 1024:1280])
    col_d = lines(rhos, cols[0], cols[1] + own_cols)
    return last(rhos, kappa, kap_rows, base, rows[0], rows[1] + own[:, :1024], col_d)


def solution(mesh):
    fine = Mesh(mesh.devices.reshape(SIZES), AXES)
    placed = P(None, ROW, COL)
    return jax.shard_map(
        shards,
        mesh=fine,
        in_specs=(placed, placed, P(), P(), P(), P()),
        out_specs=placed,
        check_vma=False,
    )
```

```python
import itertools

import jax
import jax.numpy as jnp
from jax import lax
from jax.experimental import pallas as pl
from jax.experimental.pallas import tpu as pltpu
from jax.sharding import Mesh, PartitionSpec as P

AXES = ("xl", "z", "core", "y", "xh")
SIZES = (2, 8, 2, 4, 2)
ROW = AXES[:3]
COL = AXES[3:]
PLACES = [dict(zip(AXES, place)) for place in itertools.product(*map(range, SIZES))]


LANES = 128
BLOCK = 256
MIB = 1 << 20


def flat(place):
    index = 0
    for axis, size in zip(AXES, SIZES):
        index = index * size + place[axis]
    return index


def exchange(x, role1, role0):
    pairs = []
    for p in PLACES:
        partners = (role0, role1)[p["core"]]
        if partners:
            there = {axis: partner(p[axis]) for axis, partner in partners.items()}
            pairs.append((flat(p), flat({**p, **there})))
    return lax.ppermute(x, AXES, pairs)


def across(i):
    return i ^ 1


def z_next(z):
    return (z + 1) % 8 if z % 2 else (z - 1) % 8


def z_far(z):
    return (3, 6, 5, 0, 7, 2, 1, 4)[z]


def y_next(y):
    return (y + 1) % 4 if y % 2 else (y - 1) % 4


def spot():
    row = (lax.axis_index("xl") * 8 + lax.axis_index("z")) * 2 + lax.axis_index("core")
    col = lax.axis_index("y") * 2 + lax.axis_index("xh")
    return row, col


def sides():
    xl, z, core, y, xh = (lax.axis_index(axis) for axis in AXES)
    odd = core == 1
    next_z = ((z % 2 == 0) & (z != 0)) | (z == 7)
    return (
        odd,
        jnp.where(odd, z, y) % 2 == 1,
        (odd & next_z) | (~odd & (y >= 2)),
        (z <= 2) | (z == 4),
        (z == 1) | (z == 2) | (z == 4) | (z == 7),
        xh == 0,
        xl == 1,
    )


def down_rows(ref, row):
    halves = []
    for half in range(2):
        lanes = ref[pl.ds(row * 2 + half, 1), :]
        halves.append(jnp.broadcast_to(lanes, (LANES, LANES)).T)
    return jnp.concatenate(halves, axis=0)


PIECES = (64, 64, 64, 48, 16)


def sums_kernel(
    corr_hbm, slope_hbm, kappa_hbm, detune_hbm, pump_hbm,
    sec_ref, sums_ref, kap_rows, kappa_buf, detune_ref, pump_ref, sides_ref,
    corr_buf, slope_buf, col_part, sems, small_sems,
):
    row, col = spot()
    core = lax.axis_index("core")
    kappa_copy, *late = [
        pltpu.make_async_copy(there, here, small_sems.at[n])
        for n, (there, here) in enumerate(
            ((kappa_hbm, kappa_buf), (detune_hbm, detune_ref), (pump_hbm, pump_ref))
        )
    ]
    kappa_copy.start()

    def piece(lo, rows, c):
        part = pl.ds(pl.multiple_of(lo, 8), rows)
        return (
            pltpu.make_async_copy(corr_hbm.at[:, part], corr_buf.at[:, part], sems.at[0, c]),
            pltpu.make_async_copy(slope_hbm.at[:, part], slope_buf.at[:, part], sems.at[1, c]),
        )

    @pl.loop(0, len(PIECES) - 2)
    def _(c):
        for copy in piece(c * PIECES[0], PIECES[0], c):
            copy.start()

    for c in (-2, -1):
        for copy in piece(256 - sum(PIECES[c:]), PIECES[c], len(PIECES) + c):
            copy.start()

    for copy in late:
        copy.start()
    sums_ref[:, pl.ds(1536, 512)] = jnp.zeros((2, 512), jnp.float32)
    for n, side in enumerate(sides()):
        sides_ref[n] = jnp.full((2, 1024), jnp.where(side, 1.0, 0.0))
    kappa_copy.wait()
    kap_rows[...] = down_rows(kappa_buf, row)
    kap_cols = [
        jnp.broadcast_to(kappa_buf[pl.ds(col * 8 + b, 1), :], (8, LANES)) for b in range(8)
    ]
    totals = tuple(jnp.zeros((8, LANES), jnp.float32) for _ in range(16))
    hi = 0
    for c, rows in enumerate(PIECES):
        lo, hi = hi, hi + rows
        for copy in piece(lo, rows, c):
            copy.wait()

        def group(g, totals):
            totals = list(totals)
            at = pl.ds(pl.multiple_of(lo + g * 8, 8), 8)
            kr = kap_rows[at, :]
            for p in range(2):
                along = None
                for b in range(8):
                    lanes = pl.ds(b * LANES, LANES)
                    s = corr_buf[p, at, lanes] + 0.25 * slope_buf[p, at, lanes]
                    sec_ref[p, at, lanes] = s
                    totals[p * 8 + b] = totals[p * 8 + b] + s * kr
                    w = s * kap_cols[b]
                    along = w if along is None else along + w
                col_part[p, at, :] = along
            return tuple(totals)

        totals = lax.fori_loop(0, rows // 8, group, totals, unroll=2 if rows % 16 == 0 else 1)
        if hi % LANES == 0:
            half = pl.ds(hi - LANES, LANES)
            for p in range(2):
                along = jnp.sum(col_part[p, half, :].T, axis=0, keepdims=True)
                for c in range(2):
                    sums_ref[pl.ds(p, 1), pl.ds(1024 + c * 256 + hi - LANES, LANES)] = jnp.where(
                        core == c, along, 0.0
                    )
    for p in range(2):
        for b in range(8):
            total = jnp.sum(totals[p * 8 + b], axis=0, keepdims=True)
            sums_ref[pl.ds(p, 1), pl.ds(b * LANES, LANES)] = total
    for copy in late:
        copy.wait()


def split(x):
    high = x.astype(jnp.bfloat16)
    return high, (x - high.astype(jnp.float32)).astype(jnp.bfloat16)


def table(lower):
    a = lax.broadcasted_iota(jnp.int32, (BLOCK, BLOCK), 0)
    b = lax.broadcasted_iota(jnp.int32, (BLOCK, BLOCK), 1)
    before = (b < a) if lower else (a < b)
    return jnp.where(before, 1.0, jnp.where(a == b, 0.5, 0.0)).astype(jnp.bfloat16)


def matmul(a, b):
    return jnp.dot(a, b, preferred_element_type=jnp.float32)


def twice(x):
    return jnp.concatenate([x, x], axis=1)


def along_lanes(ref, first):
    return jnp.concatenate([ref[pl.ds(first, 1), :], ref[pl.ds(first + 1, 1), :]], axis=1)


def rows_kernel(rho_ref, sec_ref, kap_rows, kappa_ref, detune_ref, pump_ref, base_ref, rho_out):
    row, col = spot()
    rho_re, rho_im = rho_ref[0], rho_ref[1]
    rho_out[0] = jnp.full((8, LANES), rho_re)
    rho_out[1] = jnp.full((8, LANES), rho_im)
    e, f = 1.0 - rho_re, -rho_im
    kr = twice(kap_rows[...])
    dr = twice(down_rows(detune_ref, row))
    pr = twice(down_rows(pump_ref, row))
    mre_r = (0.5 * rho_re) * kr * kr
    mim_r = (0.5 * rho_im) * kr * kr - dr
    lower = table(True)
    for b in range(1024 // BLOCK):
        lanes = pl.ds(b * BLOCK, BLOCK)
        kc = along_lanes(kappa_ref, col * 8 + 2 * b)
        dc = along_lanes(detune_ref, col * 8 + 2 * b)
        q = []
        for p in range(2):
            high, low = split(sec_ref[p, :, lanes] * kr)
            q.append(matmul(lower, high) + matmul(lower, low))
        s_re, s_im = sec_ref[0, :, lanes], sec_ref[1, :, lanes]
        m_re = mre_r + (0.5 * rho_re) * kc * kc
        m_im = mim_r + (dc - (0.5 * rho_im) * kc * kc)
        i = lax.broadcasted_iota(jnp.int32, (256, BLOCK), 0) + row * 256
        k = lax.broadcasted_iota(jnp.int32, (256, BLOCK), 1) + (col * 1024 + b * BLOCK)
        base_ref[0, :, lanes] = (
            m_re * s_re - m_im * s_im - kr * (e * q[0] - f * q[1]) + jnp.where(i == k, pr, 0.0)
        )
        base_ref[1, :, lanes] = m_re * s_im + m_im * s_re - kr * (e * q[1] + f * q[0])


def cols_kernel(rho_ref, sec_ref, kappa_ref, part_ref, base_ref):
    _, col = spot()
    e, f = 1.0 - rho_ref[0], rho_ref[1]
    upper = table(False)
    carry = [jnp.zeros((256, 1), jnp.float32) for _ in range(2)]
    for b in range(1024 // BLOCK):
        lanes = pl.ds(b * BLOCK, BLOCK)
        kc = along_lanes(kappa_ref, col * 8 + 2 * b)
        q = []
        for p in range(2):
            w = sec_ref[p, :, lanes] * kc
            high, low = split(w)
            q.append(matmul(high, upper) + matmul(low, upper) + carry[p])
            carry[p] = carry[p] + jnp.sum(w, axis=1, keepdims=True)
        base_ref[0, :, lanes] = part_ref[0, :, lanes] - kc * (e * q[0] - f * q[1])
        base_ref[1, :, lanes] = part_ref[1, :, lanes] - kc * (e * q[1] + f * q[0])


def carried(rho_ref, b, a, sign, height):
    rho_re, rho_im = rho_ref[0, 0:1, :], sign * rho_ref[1, 0:1, :]
    both = b[0:1] + (rho_re * a[0:1] - rho_im * a[1:2]), b[1:2] + (rho_re * a[1:2] + rho_im * a[0:1])
    return [jnp.broadcast_to(x, (height, LANES)) for x in both]


OUT_EDGES = (0, 32, 64, 128, 192, 224, 256)


def last_kernel(
    rho_ref, kappa_ref, kap_rows, base_ref, before_ref, after_ref, got_ref, own_ref, theirs_ref,
    out_hbm, out_buf, col_d, sems,
):
    _, col = spot()
    odd = lax.axis_index("core") == 1
    for half in range(2):
        at = pl.ds(half * LANES, LANES)
        there = pl.ds(256 + half * LANES, LANES)
        before = jnp.where(odd, got_ref[0, :, there], before_ref[:, at])
        after = jnp.where(odd, got_ref[1, :, there], after_ref[:, at])
        own = jnp.where(
            odd,
            own_ref[:, pl.ds(1280 + half * LANES, LANES)],
            own_ref[:, pl.ds(1024 + half * LANES, LANES)],
        )
        for p, x in enumerate(carried(rho_ref, before, after + own, -1.0, LANES)):
            col_d[p, at, :] = x.T
    kap_cols = [
        jnp.broadcast_to(kappa_ref[pl.ds(col * 8 + b, 1), :], (8, LANES)) for b in range(8)
    ]
    row_ds = []
    for b in range(8):
        at = pl.ds(b * LANES, LANES)
        theirs = theirs_ref[:, at]
        before, after = put(
            jnp.where(odd, before_ref[:, at], got_ref[0, :, at]),
            jnp.where(odd, after_ref[:, at], got_ref[1, :, at]),
            odd,
            theirs,
        )
        row_ds.append(carried(rho_ref, before, after + own_ref[:, at], 1.0, 8))
    copies = []
    for c, (lo, hi) in enumerate(zip(OUT_EDGES, OUT_EDGES[1:])):

        def group(g, carry):
            at = pl.ds(pl.multiple_of(lo + g * 8, 8), 8)
            kr = kap_rows[at, :]
            for p in range(2):
                dc = col_d[p, at, :]
                for b in range(8):
                    lanes = pl.ds(b * LANES, LANES)
                    out_buf[p, at, lanes] = base_ref[p, at, lanes] - (
                        kr * row_ds[b][p] + kap_cols[b] * dc
                    )
            return carry

        lax.fori_loop(0, (hi - lo) // 8, group, 0, unroll=2)
        part = pl.ds(lo, hi - lo)
        copy = pltpu.make_async_copy(out_buf.at[:, part], out_hbm.at[:, part], sems.at[c])
        copy.start()
        copies.append(copy)
    for copy in copies:
        copy.wait()


VM = pl.BlockSpec(memory_space=pltpu.VMEM)
SM = pl.BlockSpec(memory_space=pltpu.SMEM)
HB = pl.BlockSpec(memory_space=pltpu.HBM)
F32 = jnp.float32


def call(kernel, outs, ins, out_specs, scratch=(), alias={}, flops=0, limit=20):
    return pl.pallas_call(
        kernel,
        out_shape=outs,
        in_specs=ins,
        out_specs=out_specs,
        scratch_shapes=list(scratch),
        input_output_aliases=alias,
        cost_estimate=pl.CostEstimate(flops=flops, bytes_accessed=6 * MIB, transcendentals=0),
        compiler_params=pltpu.CompilerParams(vmem_limit_bytes=limit * MIB),
    )


def vmem(*shape):
    return pltpu.VMEM(shape, F32)


WHOLE = (2, 256, 1024)
DMA = pltpu.SemaphoreType.DMA


def sums(corr, slope, *small):
    return call(
        sums_kernel,
        [vmem(*WHOLE), vmem(2, 2048), vmem(256, 128)] + [vmem(64, 128)] * 3 + [vmem(7, 2, 1024)],
        [HB] * 5,
        [VM] * 7,
        [vmem(*WHOLE), vmem(*WHOLE), vmem(2, 256, 128), DMA((2, len(PIECES))), DMA((3,))],
    )(corr, slope, *small)


def rows_part(rho, sec, kap_rows, *small):
    return call(
        rows_kernel, [vmem(*WHOLE), vmem(2, 8, 128)], [SM] + [VM] * 5, [VM] * 2, flops=10**9
    )(rho, sec, kap_rows, *small)


def cols_part(rho, sec, kappa, part):
    return call(cols_kernel, vmem(*WHOLE), [SM] + [VM] * 3, VM, alias={3: 0}, flops=10**9)(
        rho, sec, kappa, part
    )


def last(*operands):
    return call(
        last_kernel,
        jax.ShapeDtypeStruct(WHOLE, F32),
        [VM] * 9,
        HB,
        [vmem(*WHOLE), vmem(2, 256, 128), DMA((len(OUT_EDGES) - 1,))],
    )(*operands)


def put(before, after, lower, x):
    return before + jnp.where(lower, x, 0.0), after + jnp.where(lower, 0.0, x)


def shards(corr, slope_prev, kappa, detuning, pump, rho):
    small = (v.reshape(64, 128) for v in (kappa, detuning, pump))
    held = (pltpu.with_memory_space_constraint(v, pltpu.HBM) for v in (corr, slope_prev, *small))
    sec, own, kap_rows, kappa, detune, pump, places = sums(*held)
    odd, lower1, lower2, far1, far2, xh_first, xl_last = (place > 0.5 for place in places)
    tie = lax.optimization_barrier
    other_core = {"core": across}

    theirs = exchange(own, other_core, other_core)
    chip = own + theirs
    mine = jnp.where(odd, chip[:, :1024], chip[:, 1024:])
    mine, sec = tie((mine, sec))
    got = exchange(mine, {"z": across}, {"y": across})
    base, rhos = rows_part(rho, sec, kap_rows, kappa, detune, pump)
    zero = jnp.zeros_like(mine)
    before, after = put(zero, zero, lower1, got)
    pair = mine + got
    pair, base = tie((pair, base))
    got = exchange(pair, {"z": z_next}, {"y": y_next})
    got, base = tie((got, base))
    base = cols_part(rho, sec, kappa, base)
    before, after = put(before, after, lower2, got)
    far = put(zero, zero, far1, pair)
    far = put(*far, far2, got)
    near = put(before, after, xh_first, mine)
    there = jnp.stack([jnp.where(odd, f, n) for f, n in zip(far, near)])
    got = exchange(there, {"z": z_far}, {"xh": across})
    before, after = before + got[0], after + got[1]
    line, base = tie((mine + before + after, base))
    got = exchange(line, {"xl": across}, None)
    before, after = put(before, after, xl_last, got)
    got = exchange(jnp.stack([before, after]), other_core, other_core)
    return last(rhos, kappa, kap_rows, base, before, after, got, own, theirs)


def solution(mesh):
    fine = Mesh(mesh.devices.reshape(SIZES), AXES)
    placed = P(None, ROW, COL)
    return jax.shard_map(
        shards,
        mesh=fine,
        in_specs=(placed, placed, P(), P(), P(), P()),
        out_specs=placed,
        check_vma=False,
    )
```

```python
import itertools

import jax
import jax.numpy as jnp
from jax import lax
from jax.experimental import pallas as pl
from jax.experimental.pallas import tpu as pltpu
from jax.sharding import Mesh, PartitionSpec as P

AXES = ("xl", "z", "core", "y", "xh")
SIZES = (2, 8, 2, 4, 2)
ROW = AXES[:3]
COL = AXES[3:]
PLACES = [dict(zip(AXES, place)) for place in itertools.product(*map(range, SIZES))]


LANES = 128
BLOCK = 256
MIB = 1 << 20


def flat(place):
    index = 0
    for axis, size in zip(AXES, SIZES):
        index = index * size + place[axis]
    return index


def exchange(x, role1, role0):
    pairs = []
    for p in PLACES:
        partners = (role0, role1)[p["core"]]
        if partners:
            there = {axis: partner(p[axis]) for axis, partner in partners.items()}
            pairs.append((flat(p), flat({**p, **there})))
    return lax.ppermute(x, AXES, pairs)


def across(i):
    return i ^ 1


def z_next(z):
    return (z + 1) % 8 if z % 2 else (z - 1) % 8


def z_far(z):
    return (3, 6, 5, 0, 7, 2, 1, 4)[z]


def y_next(y):
    return (y + 1) % 4 if y % 2 else (y - 1) % 4


def spot():
    row = (lax.axis_index("xl") * 8 + lax.axis_index("z")) * 2 + lax.axis_index("core")
    col = lax.axis_index("y") * 2 + lax.axis_index("xh")
    return row, col


def sides():
    xl, z, core, y, xh = (lax.axis_index(axis) for axis in AXES)
    odd = core == 1
    next_z = ((z % 2 == 0) & (z != 0)) | (z == 7)
    return (
        odd,
        jnp.where(odd, z, y) % 2 == 1,
        (odd & next_z) | (~odd & (y >= 2)),
        (z <= 2) | (z == 4),
        (z == 1) | (z == 2) | (z == 4) | (z == 7),
        xh == 0,
        xl == 1,
    )


def down_rows(ref, row):
    halves = []
    for half in range(2):
        lanes = ref[pl.ds(row * 2 + half, 1), :]
        halves.append(jnp.broadcast_to(lanes, (LANES, LANES)).T)
    return jnp.concatenate(halves, axis=0)


PIECES = (64, 64, 64, 48, 16)


def sums_kernel(
    corr_hbm, slope_hbm, kappa_hbm, detune_hbm, pump_hbm,
    sec_ref, sums_ref, kap_rows, kappa_buf, detune_ref, pump_ref, sides_ref,
    corr_buf, slope_buf, col_part, sems, small_sems,
):
    row, col = spot()
    core = lax.axis_index("core")
    kappa_copy, *late = [
        pltpu.make_async_copy(there, here, small_sems.at[n])
        for n, (there, here) in enumerate(
            ((kappa_hbm, kappa_buf), (detune_hbm, detune_ref), (pump_hbm, pump_ref))
        )
    ]
    kappa_copy.start()

    def piece(lo, rows, c):
        part = pl.ds(pl.multiple_of(lo, 8), rows)
        return (
            pltpu.make_async_copy(corr_hbm.at[:, part], corr_buf.at[:, part], sems.at[0, c]),
            pltpu.make_async_copy(slope_hbm.at[:, part], slope_buf.at[:, part], sems.at[1, c]),
        )

    @pl.loop(0, len(PIECES) - 2)
    def _(c):
        for copy in piece(c * PIECES[0], PIECES[0], c):
            copy.start()

    for c in (-2, -1):
        for copy in piece(256 - sum(PIECES[c:]), PIECES[c], len(PIECES) + c):
            copy.start()

    for copy in late:
        copy.start()
    sums_ref[:, pl.ds(1536, 512)] = jnp.zeros((2, 512), jnp.float32)
    for n, side in enumerate(sides()):
        sides_ref[n] = jnp.full((2, 1024), jnp.where(side, 1.0, 0.0))
    kappa_copy.wait()
    kap_rows[...] = down_rows(kappa_buf, row)
    kap_cols = [
        jnp.broadcast_to(kappa_buf[pl.ds(col * 8 + b, 1), :], (8, LANES)) for b in range(8)
    ]
    totals = tuple(jnp.zeros((8, LANES), jnp.float32) for _ in range(16))
    hi = 0
    for c, rows in enumerate(PIECES):
        lo, hi = hi, hi + rows
        for copy in piece(lo, rows, c):
            copy.wait()

        def group(g, totals):
            totals = list(totals)
            at = pl.ds(pl.multiple_of(lo + g * 8, 8), 8)
            kr = kap_rows[at, :]
            for p in range(2):
                along = None
                for b in range(8):
                    lanes = pl.ds(b * LANES, LANES)
                    s = corr_buf[p, at, lanes] + 0.25 * slope_buf[p, at, lanes]
                    sec_ref[p, at, lanes] = s
                    totals[p * 8 + b] = totals[p * 8 + b] + s * kr
                    w = s * kap_cols[b]
                    along = w if along is None else along + w
                col_part[p, at, :] = along
            return tuple(totals)

        totals = lax.fori_loop(0, rows // 8, group, totals, unroll=2 if rows % 16 == 0 else 1)
        if hi % LANES == 0:
            half = pl.ds(hi - LANES, LANES)
            for p in range(2):
                along = jnp.sum(col_part[p, half, :].T, axis=0, keepdims=True)
                for c in range(2):
                    sums_ref[pl.ds(p, 1), pl.ds(1024 + c * 256 + hi - LANES, LANES)] = jnp.where(
                        core == c, along, 0.0
                    )
    for p in range(2):
        for b in range(8):
            total = jnp.sum(totals[p * 8 + b], axis=0, keepdims=True)
            sums_ref[pl.ds(p, 1), pl.ds(b * LANES, LANES)] = total
    for copy in late:
        copy.wait()


def split(x):
    high = x.astype(jnp.bfloat16)
    return high, (x - high.astype(jnp.float32)).astype(jnp.bfloat16)


def table(lower):
    a = lax.broadcasted_iota(jnp.int32, (BLOCK, BLOCK), 0)
    b = lax.broadcasted_iota(jnp.int32, (BLOCK, BLOCK), 1)
    before = (b < a) if lower else (a < b)
    return jnp.where(before, 1.0, jnp.where(a == b, 0.5, 0.0)).astype(jnp.bfloat16)


def matmul(a, b):
    return jnp.dot(a, b, preferred_element_type=jnp.float32)


def twice(x):
    return jnp.concatenate([x, x], axis=1)


def along_lanes(ref, first):
    return jnp.concatenate([ref[pl.ds(first, 1), :], ref[pl.ds(first + 1, 1), :]], axis=1)


def rows_kernel(rho_ref, sec_ref, kap_rows, kappa_ref, detune_ref, pump_ref, base_ref, rho_out):
    row, col = spot()
    rho_re, rho_im = rho_ref[0], rho_ref[1]
    rho_out[0] = jnp.full((8, LANES), rho_re)
    rho_out[1] = jnp.full((8, LANES), rho_im)
    e, f = 1.0 - rho_re, -rho_im
    kr = twice(kap_rows[...])
    dr = twice(down_rows(detune_ref, row))
    pr = twice(down_rows(pump_ref, row))
    mre_r = (0.5 * rho_re) * kr * kr
    mim_r = (0.5 * rho_im) * kr * kr - dr
    lower = table(True)
    for b in range(1024 // BLOCK):
        lanes = pl.ds(b * BLOCK, BLOCK)
        kc = along_lanes(kappa_ref, col * 8 + 2 * b)
        dc = along_lanes(detune_ref, col * 8 + 2 * b)
        q = []
        for p in range(2):
            high, low = split(sec_ref[p, :, lanes] * kr)
            q.append(matmul(lower, high) + matmul(lower, low))
        s_re, s_im = sec_ref[0, :, lanes], sec_ref[1, :, lanes]
        m_re = mre_r + (0.5 * rho_re) * kc * kc
        m_im = mim_r + (dc - (0.5 * rho_im) * kc * kc)
        i = lax.broadcasted_iota(jnp.int32, (256, BLOCK), 0) + row * 256
        k = lax.broadcasted_iota(jnp.int32, (256, BLOCK), 1) + (col * 1024 + b * BLOCK)
        base_ref[0, :, lanes] = (
            m_re * s_re - m_im * s_im - kr * (e * q[0] - f * q[1]) + jnp.where(i == k, pr, 0.0)
        )
        base_ref[1, :, lanes] = m_re * s_im + m_im * s_re - kr * (e * q[1] + f * q[0])


def cols_kernel(rho_ref, sec_ref, kappa_ref, part_ref, base_ref):
    _, col = spot()
    e, f = 1.0 - rho_ref[0], rho_ref[1]
    upper = table(False)
    carry = [jnp.zeros((256, 1), jnp.float32) for _ in range(2)]
    for b in range(1024 // BLOCK):
        lanes = pl.ds(b * BLOCK, BLOCK)
        kc = along_lanes(kappa_ref, col * 8 + 2 * b)
        q = []
        for p in range(2):
            w = sec_ref[p, :, lanes] * kc
            high, low = split(w)
            q.append(matmul(high, upper) + matmul(low, upper) + carry[p])
            carry[p] = carry[p] + jnp.sum(w, axis=1, keepdims=True)
        base_ref[0, :, lanes] = part_ref[0, :, lanes] - kc * (e * q[0] - f * q[1])
        base_ref[1, :, lanes] = part_ref[1, :, lanes] - kc * (e * q[1] + f * q[0])


def carried(rho_ref, b, a, sign, height):
    rho_re, rho_im = rho_ref[0, 0:1, :], sign * rho_ref[1, 0:1, :]
    both = b[0:1] + (rho_re * a[0:1] - rho_im * a[1:2]), b[1:2] + (rho_re * a[1:2] + rho_im * a[0:1])
    return [jnp.broadcast_to(x, (height, LANES)) for x in both]


OUT_EDGES = (0, 32, 64, 128, 192, 224, 256)


def last_kernel(
    rho_ref, kappa_ref, kap_rows, base_ref, before_ref, after_ref, got_ref, own_ref, theirs_ref,
    out_hbm, out_buf, col_d, sems,
):
    _, col = spot()
    odd = lax.axis_index("core") == 1
    for half in range(2):
        at = pl.ds(half * LANES, LANES)
        there = pl.ds(256 + half * LANES, LANES)
        before = jnp.where(odd, got_ref[0, :, there], before_ref[:, at])
        after = jnp.where(odd, got_ref[1, :, there], after_ref[:, at])
        own = jnp.where(
            odd,
            own_ref[:, pl.ds(1280 + half * LANES, LANES)],
            own_ref[:, pl.ds(1024 + half * LANES, LANES)],
        )
        for p, x in enumerate(carried(rho_ref, before, after + own, -1.0, LANES)):
            col_d[p, at, :] = x.T
    kap_cols = [
        jnp.broadcast_to(kappa_ref[pl.ds(col * 8 + b, 1), :], (8, LANES)) for b in range(8)
    ]
    row_ds = []
    for b in range(8):
        at = pl.ds(b * LANES, LANES)
        theirs = theirs_ref[:, at]
        before, after = put(
            jnp.where(odd, before_ref[:, at], got_ref[0, :, at]),
            jnp.where(odd, after_ref[:, at], got_ref[1, :, at]),
            odd,
            theirs,
        )
        row_ds.append(carried(rho_ref, before, after + own_ref[:, at], 1.0, 8))
    copies = []
    for c, (lo, hi) in enumerate(zip(OUT_EDGES, OUT_EDGES[1:])):

        def group(g, carry):
            at = pl.ds(pl.multiple_of(lo + g * 8, 8), 8)
            kr = kap_rows[at, :]
            for p in range(2):
                dc = col_d[p, at, :]
                for b in range(8):
                    lanes = pl.ds(b * LANES, LANES)
                    out_buf[p, at, lanes] = base_ref[p, at, lanes] - (
                        kr * row_ds[b][p] + kap_cols[b] * dc
                    )
            return carry

        lax.fori_loop(0, (hi - lo) // 8, group, 0, unroll=2)
        part = pl.ds(lo, hi - lo)
        copy = pltpu.make_async_copy(out_buf.at[:, part], out_hbm.at[:, part], sems.at[c])
        copy.start()
        copies.append(copy)
    for copy in copies:
        copy.wait()


VM = pl.BlockSpec(memory_space=pltpu.VMEM)
SM = pl.BlockSpec(memory_space=pltpu.SMEM)
HB = pl.BlockSpec(memory_space=pltpu.HBM)
F32 = jnp.float32


def call(kernel, outs, ins, out_specs, scratch=(), alias={}, flops=0, limit=20):
    return pl.pallas_call(
        kernel,
        out_shape=outs,
        in_specs=ins,
        out_specs=out_specs,
        scratch_shapes=list(scratch),
        input_output_aliases=alias,
        cost_estimate=pl.CostEstimate(flops=flops, bytes_accessed=6 * MIB, transcendentals=0),
        compiler_params=pltpu.CompilerParams(vmem_limit_bytes=limit * MIB),
    )


def vmem(*shape):
    return pltpu.VMEM(shape, F32)


WHOLE = (2, 256, 1024)
DMA = pltpu.SemaphoreType.DMA


def sums(corr, slope, *small):
    return call(
        sums_kernel,
        [vmem(*WHOLE), vmem(2, 2048), vmem(256, 128)] + [vmem(64, 128)] * 3 + [vmem(7, 2, 1024)],
        [HB] * 5,
        [VM] * 7,
        [vmem(*WHOLE), vmem(*WHOLE), vmem(2, 256, 128), DMA((2, len(PIECES))), DMA((3,))],
    )(corr, slope, *small)


def rows_part(rho, sec, kap_rows, *small):
    return call(
        rows_kernel, [vmem(*WHOLE), vmem(2, 8, 128)], [SM] + [VM] * 5, [VM] * 2, flops=10**9
    )(rho, sec, kap_rows, *small)


def cols_part(rho, sec, kappa, part):
    return call(cols_kernel, vmem(*WHOLE), [SM] + [VM] * 3, VM, alias={3: 0}, flops=10**9)(
        rho, sec, kappa, part
    )


def last(*operands):
    return call(
        last_kernel,
        jax.ShapeDtypeStruct(WHOLE, F32),
        [VM] * 9,
        HB,
        [vmem(*WHOLE), vmem(2, 256, 128), DMA((len(OUT_EDGES) - 1,))],
    )(*operands)


def put(before, after, lower, x):
    return before + jnp.where(lower, x, 0.0), after + jnp.where(lower, 0.0, x)


def shards(corr, slope_prev, kappa, detuning, pump, rho):
    small = (v.reshape(64, 128) for v in (kappa, detuning, pump))
    held = (pltpu.with_memory_space_constraint(v, pltpu.HBM) for v in (corr, slope_prev, *small))
    sec, own, kap_rows, kappa, detune, pump, places = sums(*held)
    odd, lower1, lower2, far1, far2, xh_first, xl_last = (place > 0.5 for place in places)
    tie = lax.optimization_barrier
    other_core = {"core": across}

    theirs = exchange(own, other_core, other_core)
    chip = own + theirs
    mine = jnp.where(odd, chip[:, :1024], chip[:, 1024:])
    mine, sec = tie((mine, sec))
    got = exchange(mine, {"z": across}, {"y": across})
    base, rhos = rows_part(rho, sec, kap_rows, kappa, detune, pump)
    zero = jnp.zeros_like(mine)
    before, after = put(zero, zero, lower1, got)
    pair = mine + got
    pair, base = tie((pair, base))
    got = exchange(pair, {"z": z_next}, {"y": y_next})
    got, base = tie((got, base))
    base = cols_part(rho, sec, kappa, base)
    before, after = put(before, after, lower2, got)
    far = put(zero, zero, far1, pair)
    far = put(*far, far2, got)
    near = put(before, after, xh_first, mine)
    there = jnp.stack([jnp.where(odd, f, n) for f, n in zip(far, near)])
    got = exchange(there, {"z": z_far}, {"xl": across})
    line, base = tie((mine + before + after + got[0] + got[1], base))
    there = jnp.where(odd, line, got)
    far = got
    got = exchange(there, {"xl": across}, {"xl": across, "xh": across})
    lined = put(before + far[0], after + far[1], xl_last, got[0])
    before = jnp.where(odd, lined[0], before + got[0])
    after = jnp.where(odd, lined[1], after + got[1])
    got = exchange(jnp.stack([before, after]), other_core, other_core)
    return last(rhos, kappa, kap_rows, base, before, after, got, own, theirs)


def solution(mesh):
    fine = Mesh(mesh.devices.reshape(SIZES), AXES)
    placed = P(None, ROW, COL)
    return jax.shard_map(
        shards,
        mesh=fine,
        in_specs=(placed, placed, P(), P(), P(), P()),
        out_specs=placed,
        check_vma=False,
    )
```

```python
import itertools

import jax
import jax.numpy as jnp
from jax import lax
from jax.experimental import pallas as pl
from jax.experimental.pallas import tpu as pltpu
from jax.sharding import Mesh, PartitionSpec as P

AXES = ("xl", "z", "core", "y", "xh")
SIZES = (2, 8, 2, 4, 2)
ROW = AXES[:3]
COL = AXES[3:]
PLACES = [dict(zip(AXES, place)) for place in itertools.product(*map(range, SIZES))]


LANES = 128
BLOCK = 256
MIB = 1 << 20


def flat(place):
    index = 0
    for axis, size in zip(AXES, SIZES):
        index = index * size + place[axis]
    return index


def exchange(x, role1, role0):
    pairs = []
    for p in PLACES:
        partners = (role0, role1)[p["core"]]
        if partners:
            there = {axis: partner(p[axis]) for axis, partner in partners.items()}
            pairs.append((flat(p), flat({**p, **there})))
    return lax.ppermute(x, AXES, pairs)


def across(i):
    return i ^ 1


def z_next(z):
    return (z + 1) % 8 if z % 2 else (z - 1) % 8


def z_far(z):
    return (3, 6, 5, 0, 7, 2, 1, 4)[z]


def y_next(y):
    return (y + 1) % 4 if y % 2 else (y - 1) % 4


def spot():
    row = (lax.axis_index("xl") * 8 + lax.axis_index("z")) * 2 + lax.axis_index("core")
    col = lax.axis_index("y") * 2 + lax.axis_index("xh")
    return row, col


def sides():
    xl, z, core, y, xh = (lax.axis_index(axis) for axis in AXES)
    odd = core == 1
    next_z = ((z % 2 == 0) & (z != 0)) | (z == 7)
    return (
        odd,
        jnp.where(odd, z, y) % 2 == 1,
        (odd & next_z) | (~odd & (y >= 2)),
        (z <= 2) | (z == 4),
        (z == 1) | (z == 2) | (z == 4) | (z == 7),
        xh == 0,
        xl == 1,
    )


def down_rows(ref, row):
    halves = []
    for half in range(2):
        lanes = ref[pl.ds(row * 2 + half, 1), :]
        halves.append(jnp.broadcast_to(lanes, (LANES, LANES)).T)
    return jnp.concatenate(halves, axis=0)


PIECES = (64, 64, 64, 48, 16)


def sums_kernel(
    corr_hbm, slope_hbm, kappa_hbm, detune_hbm, pump_hbm,
    sec_ref, sums_ref, kap_rows, kappa_buf, detune_ref, pump_ref, sides_ref,
    corr_buf, slope_buf, col_part, sems, small_sems,
):
    row, col = spot()
    core = lax.axis_index("core")
    kappa_copy, *late = [
        pltpu.make_async_copy(there, here, small_sems.at[n])
        for n, (there, here) in enumerate(
            ((kappa_hbm, kappa_buf), (detune_hbm, detune_ref), (pump_hbm, pump_ref))
        )
    ]
    kappa_copy.start()

    def piece(lo, rows, c):
        part = pl.ds(pl.multiple_of(lo, 8), rows)
        return (
            pltpu.make_async_copy(corr_hbm.at[:, part], corr_buf.at[:, part], sems.at[0, c]),
            pltpu.make_async_copy(slope_hbm.at[:, part], slope_buf.at[:, part], sems.at[1, c]),
        )

    @pl.loop(0, len(PIECES) - 2)
    def _(c):
        for copy in piece(c * PIECES[0], PIECES[0], c):
            copy.start()

    for c in (-2, -1):
        for copy in piece(256 - sum(PIECES[c:]), PIECES[c], len(PIECES) + c):
            copy.start()

    for copy in late:
        copy.start()
    sums_ref[:, pl.ds(1536, 512)] = jnp.zeros((2, 512), jnp.float32)
    for n, side in enumerate(sides()):
        sides_ref[n] = jnp.full((2, 1024), jnp.where(side, 1.0, 0.0))
    kappa_copy.wait()
    kap_rows[...] = down_rows(kappa_buf, row)
    kap_cols = [
        jnp.broadcast_to(kappa_buf[pl.ds(col * 8 + b, 1), :], (8, LANES)) for b in range(8)
    ]
    totals = tuple(jnp.zeros((8, LANES), jnp.float32) for _ in range(16))
    hi = 0
    for c, rows in enumerate(PIECES):
        lo, hi = hi, hi + rows
        for copy in piece(lo, rows, c):
            copy.wait()

        def group(g, totals):
            totals = list(totals)
            at = pl.ds(pl.multiple_of(lo + g * 8, 8), 8)
            kr = kap_rows[at, :]
            for p in range(2):
                along = None
                for b in range(8):
                    lanes = pl.ds(b * LANES, LANES)
                    s = corr_buf[p, at, lanes] + 0.25 * slope_buf[p, at, lanes]
                    sec_ref[p, at, lanes] = s
                    totals[p * 8 + b] = totals[p * 8 + b] + s * kr
                    w = s * kap_cols[b]
                    along = w if along is None else along + w
                col_part[p, at, :] = along
            return tuple(totals)

        totals = lax.fori_loop(0, rows // 8, group, totals, unroll=2 if rows % 16 == 0 else 1)
        if hi % LANES == 0:
            half = pl.ds(hi - LANES, LANES)
            for p in range(2):
                along = jnp.sum(col_part[p, half, :].T, axis=0, keepdims=True)
                for c in range(2):
                    sums_ref[pl.ds(p, 1), pl.ds(1024 + c * 256 + hi - LANES, LANES)] = jnp.where(
                        core == c, along, 0.0
                    )
    for p in range(2):
        for b in range(8):
            total = jnp.sum(totals[p * 8 + b], axis=0, keepdims=True)
            sums_ref[pl.ds(p, 1), pl.ds(b * LANES, LANES)] = total
    for copy in late:
        copy.wait()


def split(x):
    high = x.astype(jnp.bfloat16)
    return high, (x - high.astype(jnp.float32)).astype(jnp.bfloat16)


def table(lower):
    a = lax.broadcasted_iota(jnp.int32, (BLOCK, BLOCK), 0)
    b = lax.broadcasted_iota(jnp.int32, (BLOCK, BLOCK), 1)
    before = (b < a) if lower else (a < b)
    return jnp.where(before, 1.0, jnp.where(a == b, 0.5, 0.0)).astype(jnp.bfloat16)


def matmul(a, b):
    return jnp.dot(a, b, preferred_element_type=jnp.float32)


def twice(x):
    return jnp.concatenate([x, x], axis=1)


def along_lanes(ref, first):
    return jnp.concatenate([ref[pl.ds(first, 1), :], ref[pl.ds(first + 1, 1), :]], axis=1)


def rows_kernel(rho_ref, sec_ref, kap_rows, kappa_ref, detune_ref, pump_ref, base_ref, rho_out):
    row, col = spot()
    rho_re, rho_im = rho_ref[0], rho_ref[1]
    rho_out[0] = jnp.full((8, LANES), rho_re)
    rho_out[1] = jnp.full((8, LANES), rho_im)
    e, f = 1.0 - rho_re, -rho_im
    kr = twice(kap_rows[...])
    dr = twice(down_rows(detune_ref, row))
    pr = twice(down_rows(pump_ref, row))
    mre_r = (0.5 * rho_re) * kr * kr
    mim_r = (0.5 * rho_im) * kr * kr - dr
    lower = table(True)
    for b in range(1024 // BLOCK):
        lanes = pl.ds(b * BLOCK, BLOCK)
        kc = along_lanes(kappa_ref, col * 8 + 2 * b)
        dc = along_lanes(detune_ref, col * 8 + 2 * b)
        q = []
        for p in range(2):
            high, low = split(sec_ref[p, :, lanes] * kr)
            q.append(matmul(lower, high) + matmul(lower, low))
        s_re, s_im = sec_ref[0, :, lanes], sec_ref[1, :, lanes]
        m_re = mre_r + (0.5 * rho_re) * kc * kc
        m_im = mim_r + (dc - (0.5 * rho_im) * kc * kc)
        i = lax.broadcasted_iota(jnp.int32, (256, BLOCK), 0) + row * 256
        k = lax.broadcasted_iota(jnp.int32, (256, BLOCK), 1) + (col * 1024 + b * BLOCK)
        base_ref[0, :, lanes] = (
            m_re * s_re - m_im * s_im - kr * (e * q[0] - f * q[1]) + jnp.where(i == k, pr, 0.0)
        )
        base_ref[1, :, lanes] = m_re * s_im + m_im * s_re - kr * (e * q[1] + f * q[0])


def cols_kernel(rho_ref, sec_ref, kappa_ref, part_ref, base_ref):
    _, col = spot()
    e, f = 1.0 - rho_ref[0], rho_ref[1]
    upper = table(False)
    carry = [jnp.zeros((256, 1), jnp.float32) for _ in range(2)]
    for b in range(1024 // BLOCK):
        lanes = pl.ds(b * BLOCK, BLOCK)
        kc = along_lanes(kappa_ref, col * 8 + 2 * b)
        q = []
        for p in range(2):
            w = sec_ref[p, :, lanes] * kc
            high, low = split(w)
            q.append(matmul(high, upper) + matmul(low, upper) + carry[p])
            carry[p] = carry[p] + jnp.sum(w, axis=1, keepdims=True)
        base_ref[0, :, lanes] = part_ref[0, :, lanes] - kc * (e * q[0] - f * q[1])
        base_ref[1, :, lanes] = part_ref[1, :, lanes] - kc * (e * q[1] + f * q[0])


def carried(rho_ref, b, a, sign, height):
    rho_re, rho_im = rho_ref[0, 0:1, :], sign * rho_ref[1, 0:1, :]
    both = b[0:1] + (rho_re * a[0:1] - rho_im * a[1:2]), b[1:2] + (rho_re * a[1:2] + rho_im * a[0:1])
    return [jnp.broadcast_to(x, (height, LANES)) for x in both]


OUT_EDGES = (0, 32, 64, 128, 192, 224, 256)


def last_kernel(
    rho_ref, kappa_ref, kap_rows, base_ref, before_ref, after_ref, got_ref, own_ref, theirs_ref,
    out_hbm, out_buf, col_d, sems,
):
    _, col = spot()
    odd = lax.axis_index("core") == 1
    for half in range(2):
        at = pl.ds(half * LANES, LANES)
        there = pl.ds(256 + half * LANES, LANES)
        before = jnp.where(odd, got_ref[0, :, there], before_ref[:, at])
        after = jnp.where(odd, got_ref[1, :, there], after_ref[:, at])
        own = jnp.where(
            odd,
            own_ref[:, pl.ds(1280 + half * LANES, LANES)],
            own_ref[:, pl.ds(1024 + half * LANES, LANES)],
        )
        for p, x in enumerate(carried(rho_ref, before, after + own, -1.0, LANES)):
            col_d[p, at, :] = x.T
    kap_cols = [
        jnp.broadcast_to(kappa_ref[pl.ds(col * 8 + b, 1), :], (8, LANES)) for b in range(8)
    ]
    row_ds = []
    for b in range(8):
        at = pl.ds(b * LANES, LANES)
        theirs = theirs_ref[:, at]
        before, after = put(
            jnp.where(odd, before_ref[:, at], got_ref[0, :, at]),
            jnp.where(odd, after_ref[:, at], got_ref[1, :, at]),
            odd,
            theirs,
        )
        row_ds.append(carried(rho_ref, before, after + own_ref[:, at], 1.0, 8))
    copies = []
    for c, (lo, hi) in enumerate(zip(OUT_EDGES, OUT_EDGES[1:])):

        def group(g, carry):
            at = pl.ds(pl.multiple_of(lo + g * 8, 8), 8)
            kr = kap_rows[at, :]
            for p in range(2):
                dc = col_d[p, at, :]
                for b in range(8):
                    lanes = pl.ds(b * LANES, LANES)
                    out_buf[p, at, lanes] = base_ref[p, at, lanes] - (
                        kr * row_ds[b][p] + kap_cols[b] * dc
                    )
            return carry

        lax.fori_loop(0, (hi - lo) // 8, group, 0, unroll=2)
        part = pl.ds(lo, hi - lo)
        copy = pltpu.make_async_copy(out_buf.at[:, part], out_hbm.at[:, part], sems.at[c])
        copy.start()
        copies.append(copy)
    for copy in copies:
        copy.wait()


VM = pl.BlockSpec(memory_space=pltpu.VMEM)
SM = pl.BlockSpec(memory_space=pltpu.SMEM)
HB = pl.BlockSpec(memory_space=pltpu.HBM)
F32 = jnp.float32


def call(kernel, outs, ins, out_specs, scratch=(), alias={}, flops=0, limit=20):
    return pl.pallas_call(
        kernel,
        out_shape=outs,
        in_specs=ins,
        out_specs=out_specs,
        scratch_shapes=list(scratch),
        input_output_aliases=alias,
        cost_estimate=pl.CostEstimate(flops=flops, bytes_accessed=6 * MIB, transcendentals=0),
        compiler_params=pltpu.CompilerParams(vmem_limit_bytes=limit * MIB),
    )


def vmem(*shape):
    return pltpu.VMEM(shape, F32)


WHOLE = (2, 256, 1024)
DMA = pltpu.SemaphoreType.DMA


def sums(corr, slope, *small):
    return call(
        sums_kernel,
        [vmem(*WHOLE), vmem(2, 2048), vmem(256, 128)] + [vmem(64, 128)] * 3 + [vmem(7, 2, 1024)],
        [HB] * 5,
        [VM] * 7,
        [vmem(*WHOLE), vmem(*WHOLE), vmem(2, 256, 128), DMA((2, len(PIECES))), DMA((3,))],
    )(corr, slope, *small)


def rows_part(rho, sec, kap_rows, *small):
    return call(
        rows_kernel, [vmem(*WHOLE), vmem(2, 8, 128)], [SM] + [VM] * 5, [VM] * 2, flops=10**9
    )(rho, sec, kap_rows, *small)


def cols_part(rho, sec, kappa, part):
    return call(cols_kernel, vmem(*WHOLE), [SM] + [VM] * 3, VM, alias={3: 0}, flops=10**9)(
        rho, sec, kappa, part
    )


def last(*operands):
    return call(
        last_kernel,
        jax.ShapeDtypeStruct(WHOLE, F32),
        [VM] * 9,
        HB,
        [vmem(*WHOLE), vmem(2, 256, 128), DMA((len(OUT_EDGES) - 1,))],
    )(*operands)


def put(before, after, lower, x):
    return before + jnp.where(lower, x, 0.0), after + jnp.where(lower, 0.0, x)


def shards(corr, slope_prev, kappa, detuning, pump, rho):
    small = (v.reshape(64, 128) for v in (kappa, detuning, pump))
    held = (pltpu.with_memory_space_constraint(v, pltpu.HBM) for v in (corr, slope_prev, *small))
    sec, own, kap_rows, kappa, detune, pump, places = sums(*held)
    odd, lower1, lower2, far1, far2, xh_first, xl_last = (place > 0.5 for place in places)
    tie = lax.optimization_barrier
    other_core = {"core": across}

    theirs = exchange(own, other_core, other_core)
    chip = own + theirs
    mine = jnp.where(odd, chip[:, :1024], chip[:, 1024:])
    mine, sec = tie((mine, sec))
    got = exchange(mine, {"z": across}, {"y": across})
    base, rhos = rows_part(rho, sec, kap_rows, kappa, detune, pump)
    zero = jnp.zeros_like(mine)
    before, after = put(zero, zero, lower1, got)
    pair = mine + got
    pair, base = tie((pair, base))
    got = exchange(pair, {"z": z_next}, None)
    before, after = put(before, after, lower2, got)
    far = put(zero, zero, far1, pair)
    far = put(*far, far2, got)
    there = jnp.stack([jnp.where(odd, f, pair) for f in far])
    there, base = tie((there, base))
    got = exchange(there, {"z": z_far}, {"y": y_next})
    base = cols_part(rho, sec, kappa, base)
    got, base = tie((got, base))
    lined = put(before, after, lower2, got[0])
    before = jnp.where(odd, before + got[0], lined[0])
    after = jnp.where(odd, after + got[1], lined[1])
    near = put(before, after, xh_first, mine)
    there = jnp.stack([jnp.where(odd, mine + before + after, n) for n in near])
    got = exchange(there, {"xl": across}, {"xh": across})
    lined = put(before, after, xl_last, got[0])
    before = jnp.where(odd, lined[0], before + got[0])
    after = jnp.where(odd, lined[1], after + got[1])
    got = exchange(jnp.stack([before, after]), other_core, other_core)
    return last(rhos, kappa, kap_rows, base, before, after, got, own, theirs)


def solution(mesh):
    fine = Mesh(mesh.devices.reshape(SIZES), AXES)
    placed = P(None, ROW, COL)
    return jax.shard_map(
        shards,
        mesh=fine,
        in_specs=(placed, placed, P(), P(), P(), P()),
        out_specs=placed,
        check_vma=False,
    )
```

```python
import itertools

import jax
import jax.numpy as jnp
from jax import lax
from jax.experimental import pallas as pl
from jax.experimental.pallas import tpu as pltpu
from jax.sharding import Mesh, PartitionSpec as P

AXES = ("xl", "z", "core", "y", "xh")
SIZES = (2, 8, 2, 4, 2)
ROW = AXES[:3]
COL = AXES[3:]
PLACES = [dict(zip(AXES, place)) for place in itertools.product(*map(range, SIZES))]


LANES = 128
BLOCK = 256
MIB = 1 << 20


def flat(place):
    index = 0
    for axis, size in zip(AXES, SIZES):
        index = index * size + place[axis]
    return index


def exchange(x, role1, role0):
    pairs = []
    for p in PLACES:
        partners = (role0, role1)[p["core"]]
        if partners:
            there = {axis: partner(p[axis]) for axis, partner in partners.items()}
            pairs.append((flat(p), flat({**p, **there})))
    return lax.ppermute(x, AXES, pairs)


def across(i):
    return i ^ 1


def z_next(z):
    return (z + 1) % 8 if z % 2 else (z - 1) % 8


def z_far(z):
    return (3, 6, 5, 0, 7, 2, 1, 4)[z]


def y_next(y):
    return (y + 1) % 4 if y % 2 else (y - 1) % 4


def spot():
    row = (lax.axis_index("xl") * 8 + lax.axis_index("z")) * 2 + lax.axis_index("core")
    col = lax.axis_index("y") * 2 + lax.axis_index("xh")
    return row, col


def sides():
    xl, z, core, y, xh = (lax.axis_index(axis) for axis in AXES)
    odd = core == 1
    next_z = ((z % 2 == 0) & (z != 0)) | (z == 7)
    return (
        odd,
        z % 2 == 1,
        (odd & next_z) | (~odd & (xh == 1)),
        (z <= 2) | (z == 4),
        (z == 1) | (z == 2) | (z == 4) | (z == 7),
        y % 2 == 1,
        (odd & (xl == 1)) | (~odd & (y >= 2)),
    )


def down_rows(ref, row):
    halves = []
    for half in range(2):
        lanes = ref[pl.ds(row * 2 + half, 1), :]
        halves.append(jnp.broadcast_to(lanes, (LANES, LANES)).T)
    return jnp.concatenate(halves, axis=0)


PIECES = (64, 64, 64, 48, 16)


def sums_kernel(
    corr_hbm, slope_hbm, kappa_hbm, detune_hbm, pump_hbm,
    sec_ref, sums_ref, kap_rows, kappa_buf, detune_ref, pump_ref, sides_ref,
    corr_buf, slope_buf, col_part, sems, small_sems,
):
    row, col = spot()
    core = lax.axis_index("core")
    kappa_copy, *late = [
        pltpu.make_async_copy(there, here, small_sems.at[n])
        for n, (there, here) in enumerate(
            ((kappa_hbm, kappa_buf), (detune_hbm, detune_ref), (pump_hbm, pump_ref))
        )
    ]
    kappa_copy.start()

    def piece(lo, rows, c):
        part = pl.ds(pl.multiple_of(lo, 8), rows)
        return (
            pltpu.make_async_copy(corr_hbm.at[:, part], corr_buf.at[:, part], sems.at[0, c]),
            pltpu.make_async_copy(slope_hbm.at[:, part], slope_buf.at[:, part], sems.at[1, c]),
        )

    @pl.loop(0, len(PIECES) - 2)
    def _(c):
        for copy in piece(c * PIECES[0], PIECES[0], c):
            copy.start()

    for c in (-2, -1):
        for copy in piece(256 - sum(PIECES[c:]), PIECES[c], len(PIECES) + c):
            copy.start()

    for copy in late:
        copy.start()
    sums_ref[:, pl.ds(1536, 512)] = jnp.zeros((2, 512), jnp.float32)
    for n, side in enumerate(sides()):
        sides_ref[n] = jnp.full((2, 1024), jnp.where(side, 1.0, 0.0))
    kappa_copy.wait()
    kap_rows[...] = down_rows(kappa_buf, row)
    kap_cols = [
        jnp.broadcast_to(kappa_buf[pl.ds(col * 8 + b, 1), :], (8, LANES)) for b in range(8)
    ]
    totals = tuple(jnp.zeros((8, LANES), jnp.float32) for _ in range(16))
    hi = 0
    for c, rows in enumerate(PIECES):
        lo, hi = hi, hi + rows
        for copy in piece(lo, rows, c):
            copy.wait()

        def group(g, totals):
            totals = list(totals)
            at = pl.ds(pl.multiple_of(lo + g * 8, 8), 8)
            kr = kap_rows[at, :]
            for p in range(2):
                along = None
                for b in range(8):
                    lanes = pl.ds(b * LANES, LANES)
                    s = corr_buf[p, at, lanes] + 0.25 * slope_buf[p, at, lanes]
                    sec_ref[p, at, lanes] = s
                    totals[p * 8 + b] = totals[p * 8 + b] + s * kr
                    w = s * kap_cols[b]
                    along = w if along is None else along + w
                col_part[p, at, :] = along
            return tuple(totals)

        totals = lax.fori_loop(0, rows // 8, group, totals, unroll=2 if rows % 16 == 0 else 1)
        if hi % LANES == 0:
            half = pl.ds(hi - LANES, LANES)
            for p in range(2):
                along = jnp.sum(col_part[p, half, :].T, axis=0, keepdims=True)
                for c in range(2):
                    sums_ref[pl.ds(p, 1), pl.ds(1024 + c * 256 + hi - LANES, LANES)] = jnp.where(
                        core == c, along, 0.0
                    )
    for p in range(2):
        for b in range(8):
            total = jnp.sum(totals[p * 8 + b], axis=0, keepdims=True)
            sums_ref[pl.ds(p, 1), pl.ds(b * LANES, LANES)] = total
    for copy in late:
        copy.wait()


def split(x):
    high = x.astype(jnp.bfloat16)
    return high, (x - high.astype(jnp.float32)).astype(jnp.bfloat16)


def table(lower):
    a = lax.broadcasted_iota(jnp.int32, (BLOCK, BLOCK), 0)
    b = lax.broadcasted_iota(jnp.int32, (BLOCK, BLOCK), 1)
    before = (b < a) if lower else (a < b)
    return jnp.where(before, 1.0, jnp.where(a == b, 0.5, 0.0)).astype(jnp.bfloat16)


def matmul(a, b):
    return jnp.dot(a, b, preferred_element_type=jnp.float32)


def twice(x):
    return jnp.concatenate([x, x], axis=1)


def along_lanes(ref, first):
    return jnp.concatenate([ref[pl.ds(first, 1), :], ref[pl.ds(first + 1, 1), :]], axis=1)


def rows_kernel(rho_ref, sec_ref, kap_rows, kappa_ref, detune_ref, pump_ref, base_ref, rho_out):
    row, col = spot()
    rho_re, rho_im = rho_ref[0], rho_ref[1]
    rho_out[0] = jnp.full((8, LANES), rho_re)
    rho_out[1] = jnp.full((8, LANES), rho_im)
    e, f = 1.0 - rho_re, -rho_im
    kr = twice(kap_rows[...])
    dr = twice(down_rows(detune_ref, row))
    pr = twice(down_rows(pump_ref, row))
    mre_r = (0.5 * rho_re) * kr * kr
    mim_r = (0.5 * rho_im) * kr * kr - dr
    lower = table(True)
    for b in range(1024 // BLOCK):
        lanes = pl.ds(b * BLOCK, BLOCK)
        kc = along_lanes(kappa_ref, col * 8 + 2 * b)
        dc = along_lanes(detune_ref, col * 8 + 2 * b)
        q = []
        for p in range(2):
            high, low = split(sec_ref[p, :, lanes] * kr)
            q.append(matmul(lower, high) + matmul(lower, low))
        s_re, s_im = sec_ref[0, :, lanes], sec_ref[1, :, lanes]
        m_re = mre_r + (0.5 * rho_re) * kc * kc
        m_im = mim_r + (dc - (0.5 * rho_im) * kc * kc)
        i = lax.broadcasted_iota(jnp.int32, (256, BLOCK), 0) + row * 256
        k = lax.broadcasted_iota(jnp.int32, (256, BLOCK), 1) + (col * 1024 + b * BLOCK)
        base_ref[0, :, lanes] = (
            m_re * s_re - m_im * s_im - kr * (e * q[0] - f * q[1]) + jnp.where(i == k, pr, 0.0)
        )
        base_ref[1, :, lanes] = m_re * s_im + m_im * s_re - kr * (e * q[1] + f * q[0])


def cols_kernel(rho_ref, sec_ref, kappa_ref, part_ref, base_ref):
    _, col = spot()
    e, f = 1.0 - rho_ref[0], rho_ref[1]
    upper = table(False)
    carry = [jnp.zeros((256, 1), jnp.float32) for _ in range(2)]
    for b in range(1024 // BLOCK):
        lanes = pl.ds(b * BLOCK, BLOCK)
        kc = along_lanes(kappa_ref, col * 8 + 2 * b)
        q = []
        for p in range(2):
            w = sec_ref[p, :, lanes] * kc
            high, low = split(w)
            q.append(matmul(high, upper) + matmul(low, upper) + carry[p])
            carry[p] = carry[p] + jnp.sum(w, axis=1, keepdims=True)
        base_ref[0, :, lanes] = part_ref[0, :, lanes] - kc * (e * q[0] - f * q[1])
        base_ref[1, :, lanes] = part_ref[1, :, lanes] - kc * (e * q[1] + f * q[0])


def carried(rho_ref, b, a, sign, height):
    rho_re, rho_im = rho_ref[0, 0:1, :], sign * rho_ref[1, 0:1, :]
    both = b[0:1] + (rho_re * a[0:1] - rho_im * a[1:2]), b[1:2] + (rho_re * a[1:2] + rho_im * a[0:1])
    return [jnp.broadcast_to(x, (height, LANES)) for x in both]


OUT_EDGES = (0, 32, 64, 128, 192, 224, 256)


def last_kernel(
    rho_ref, kappa_ref, kap_rows, base_ref, before_ref, after_ref, got_ref, own_ref, theirs_ref,
    out_hbm, out_buf, col_d, sems,
):
    _, col = spot()
    odd = lax.axis_index("core") == 1
    for half in range(2):
        at = pl.ds(half * LANES, LANES)
        there = pl.ds(256 + half * LANES, LANES)
        before = jnp.where(odd, got_ref[0, :, there], before_ref[:, at])
        after = jnp.where(odd, got_ref[1, :, there], after_ref[:, at])
        own = jnp.where(
            odd,
            own_ref[:, pl.ds(1280 + half * LANES, LANES)],
            own_ref[:, pl.ds(1024 + half * LANES, LANES)],
        )
        for p, x in enumerate(carried(rho_ref, before, after + own, -1.0, LANES)):
            col_d[p, at, :] = x.T
    kap_cols = [
        jnp.broadcast_to(kappa_ref[pl.ds(col * 8 + b, 1), :], (8, LANES)) for b in range(8)
    ]
    row_ds = []
    for b in range(8):
        at = pl.ds(b * LANES, LANES)
        theirs = theirs_ref[:, at]
        before, after = put(
            jnp.where(odd, before_ref[:, at], got_ref[0, :, at]),
            jnp.where(odd, after_ref[:, at], got_ref[1, :, at]),
            odd,
            theirs,
        )
        row_ds.append(carried(rho_ref, before, after + own_ref[:, at], 1.0, 8))
    copies = []
    for c, (lo, hi) in enumerate(zip(OUT_EDGES, OUT_EDGES[1:])):

        def group(g, carry):
            at = pl.ds(pl.multiple_of(lo + g * 8, 8), 8)
            kr = kap_rows[at, :]
            for p in range(2):
                dc = col_d[p, at, :]
                for b in range(8):
                    lanes = pl.ds(b * LANES, LANES)
                    out_buf[p, at, lanes] = base_ref[p, at, lanes] - (
                        kr * row_ds[b][p] + kap_cols[b] * dc
                    )
            return carry

        lax.fori_loop(0, (hi - lo) // 8, group, 0, unroll=2)
        part = pl.ds(lo, hi - lo)
        copy = pltpu.make_async_copy(out_buf.at[:, part], out_hbm.at[:, part], sems.at[c])
        copy.start()
        copies.append(copy)
    for copy in copies:
        copy.wait()


VM = pl.BlockSpec(memory_space=pltpu.VMEM)
SM = pl.BlockSpec(memory_space=pltpu.SMEM)
HB = pl.BlockSpec(memory_space=pltpu.HBM)
F32 = jnp.float32


def call(kernel, outs, ins, out_specs, scratch=(), alias={}, flops=0, limit=20):
    return pl.pallas_call(
        kernel,
        out_shape=outs,
        in_specs=ins,
        out_specs=out_specs,
        scratch_shapes=list(scratch),
        input_output_aliases=alias,
        cost_estimate=pl.CostEstimate(flops=flops, bytes_accessed=6 * MIB, transcendentals=0),
        compiler_params=pltpu.CompilerParams(vmem_limit_bytes=limit * MIB),
    )


def vmem(*shape):
    return pltpu.VMEM(shape, F32)


WHOLE = (2, 256, 1024)
DMA = pltpu.SemaphoreType.DMA


def sums(corr, slope, *small):
    return call(
        sums_kernel,
        [vmem(*WHOLE), vmem(2, 2048), vmem(256, 128)] + [vmem(64, 128)] * 3 + [vmem(7, 2, 1024)],
        [HB] * 5,
        [VM] * 7,
        [vmem(*WHOLE), vmem(*WHOLE), vmem(2, 256, 128), DMA((2, len(PIECES))), DMA((3,))],
    )(corr, slope, *small)


def rows_part(rho, sec, kap_rows, *small):
    return call(
        rows_kernel, [vmem(*WHOLE), vmem(2, 8, 128)], [SM] + [VM] * 5, [VM] * 2, flops=10**9
    )(rho, sec, kap_rows, *small)


def cols_part(rho, sec, kappa, part):
    return call(cols_kernel, vmem(*WHOLE), [SM] + [VM] * 3, VM, alias={3: 0}, flops=10**9)(
        rho, sec, kappa, part
    )


def last(*operands):
    return call(
        last_kernel,
        jax.ShapeDtypeStruct(WHOLE, F32),
        [VM] * 9,
        HB,
        [vmem(*WHOLE), vmem(2, 256, 128), DMA((len(OUT_EDGES) - 1,))],
    )(*operands)


def put(before, after, lower, x):
    return before + jnp.where(lower, x, 0.0), after + jnp.where(lower, 0.0, x)


def shards(corr, slope_prev, kappa, detuning, pump, rho):
    small = (v.reshape(64, 128) for v in (kappa, detuning, pump))
    held = (pltpu.with_memory_space_constraint(v, pltpu.HBM) for v in (corr, slope_prev, *small))
    sec, own, kap_rows, kappa, detune, pump, places = sums(*held)
    odd, lower1, lower2, far1, far2, lower3, lower4 = (place > 0.5 for place in places)
    tie = lax.optimization_barrier
    other_core = {"core": across}

    theirs = exchange(own, other_core, other_core)
    chip = own + theirs
    mine = jnp.where(odd, chip[:, :1024], chip[:, 1024:])
    mine, sec = tie((mine, sec))
    got = exchange(mine, {"z": across}, {"xl": across})
    base, rhos = rows_part(rho, sec, kap_rows, kappa, detune, pump)
    zero = jnp.zeros_like(mine)
    before, after = put(zero, zero, lower1, jnp.where(odd, got, 0.0))
    pair = jnp.where(odd, mine + got, got)
    pair, base = tie((pair, base))
    got = exchange(pair, {"z": z_next}, {"xl": across, "xh": across})
    got, base = tie((got, base))
    base = cols_part(rho, sec, kappa, base)
    before, after = put(before, after, lower2, got)
    far = put(zero, zero, far1, pair)
    far = put(*far, far2, got)
    there = jnp.stack([jnp.where(odd, f, mine + got) for f in far])
    past = jnp.where(odd, 0.0, mine + got)
    got = exchange(there, {"z": z_far}, {"y": across})
    lined = put(before, after, lower3, got[0])
    before = jnp.where(odd, before + got[0], lined[0])
    after = jnp.where(odd, after + got[1], lined[1])
    line, base = tie((jnp.where(odd, mine + before + after, past + got[0]), base))
    got = exchange(line, {"xl": across}, {"y": y_next})
    before, after = put(before, after, lower4, got)
    got = exchange(jnp.stack([before, after]), other_core, other_core)
    return last(rhos, kappa, kap_rows, base, before, after, got, own, theirs)


def solution(mesh):
    fine = Mesh(mesh.devices.reshape(SIZES), AXES)
    placed = P(None, ROW, COL)
    return jax.shard_map(
        shards,
        mesh=fine,
        in_specs=(placed, placed, P(), P(), P(), P()),
        out_specs=placed,
        check_vma=False,
    )
```

```python
import itertools

import jax
import jax.numpy as jnp
from jax import lax
from jax.experimental import pallas as pl
from jax.experimental.pallas import tpu as pltpu
from jax.sharding import Mesh, PartitionSpec as P

AXES = ("xl", "z", "core", "y", "xh")
SIZES = (2, 8, 2, 4, 2)
ROW = AXES[:3]
COL = AXES[3:]
PLACES = [dict(zip(AXES, place)) for place in itertools.product(*map(range, SIZES))]


LANES = 128
BLOCK = 256
MIB = 1 << 20


def flat(place):
    index = 0
    for axis, size in zip(AXES, SIZES):
        index = index * size + place[axis]
    return index


def exchange(x, role1, role0):
    pairs = []
    for p in PLACES:
        partners = (role0, role1)[p["core"]]
        if partners:
            there = {axis: partner(p[axis]) for axis, partner in partners.items()}
            pairs.append((flat(p), flat({**p, **there})))
    return lax.ppermute(x, AXES, pairs)


def across(i):
    return i ^ 1


def z_next(z):
    return (z + 1) % 8 if z % 2 else (z - 1) % 8


def z_far(z):
    return (3, 6, 5, 0, 7, 2, 1, 4)[z]


def y_next(y):
    return (y + 1) % 4 if y % 2 else (y - 1) % 4


def spot():
    row = (lax.axis_index("xl") * 8 + lax.axis_index("z")) * 2 + lax.axis_index("core")
    col = lax.axis_index("y") * 2 + lax.axis_index("xh")
    return row, col


def sides():
    xl, z, core, y, xh = (lax.axis_index(axis) for axis in AXES)
    odd = core == 1
    next_z = ((z % 2 == 0) & (z != 0)) | (z == 7)
    return (
        odd,
        jnp.where(odd, z, y) % 2 == 1,
        (odd & next_z) | (~odd & (y >= 2)),
        (z <= 2) | (z == 4),
        (z == 1) | (z == 2) | (z == 4) | (z == 7),
        xh == 0,
        xl == 1,
    )


def down_rows(ref, row):
    halves = []
    for half in range(2):
        lanes = ref[pl.ds(row * 2 + half, 1), :]
        halves.append(jnp.broadcast_to(lanes, (LANES, LANES)).T)
    return jnp.concatenate(halves, axis=0)


PIECES = (64, 64, 64, 48, 16)


def sums_kernel(
    corr_hbm, slope_hbm, kappa_hbm, detune_hbm, pump_hbm,
    sec_ref, sums_ref, kap_rows, kappa_buf, detune_ref, pump_ref, sides_ref,
    corr_buf, slope_buf, col_part, sems, small_sems,
):
    row, col = spot()
    core = lax.axis_index("core")
    kappa_copy, *late = [
        pltpu.make_async_copy(there, here, small_sems.at[n])
        for n, (there, here) in enumerate(
            ((kappa_hbm, kappa_buf), (detune_hbm, detune_ref), (pump_hbm, pump_ref))
        )
    ]
    kappa_copy.start()

    def piece(lo, rows, c):
        part = pl.ds(pl.multiple_of(lo, 8), rows)
        return (
            pltpu.make_async_copy(corr_hbm.at[:, part], corr_buf.at[:, part], sems.at[0, c]),
            pltpu.make_async_copy(slope_hbm.at[:, part], slope_buf.at[:, part], sems.at[1, c]),
        )

    @pl.loop(0, len(PIECES) - 2)
    def _(c):
        for copy in piece(c * PIECES[0], PIECES[0], c):
            copy.start()

    for c in (-2, -1):
        for copy in piece(256 - sum(PIECES[c:]), PIECES[c], len(PIECES) + c):
            copy.start()

    for copy in late:
        copy.start()
    sums_ref[:, pl.ds(1536, 512)] = jnp.zeros((2, 512), jnp.float32)
    for n, side in enumerate(sides()):
        sides_ref[n] = jnp.full((2, 1024), jnp.where(side, 1.0, 0.0))
    kappa_copy.wait()
    kap_rows[...] = down_rows(kappa_buf, row)
    kap_cols = [
        jnp.broadcast_to(kappa_buf[pl.ds(col * 8 + b, 1), :], (8, LANES)) for b in range(8)
    ]
    totals = tuple(jnp.zeros((8, LANES), jnp.float32) for _ in range(16))
    hi = 0
    for c, rows in enumerate(PIECES):
        lo, hi = hi, hi + rows
        for copy in piece(lo, rows, c):
            copy.wait()

        def group(g, totals):
            totals = list(totals)
            at = pl.ds(pl.multiple_of(lo + g * 8, 8), 8)
            kr = kap_rows[at, :]
            for p in range(2):
                along = None
                for b in range(8):
                    lanes = pl.ds(b * LANES, LANES)
                    s = corr_buf[p, at, lanes] + 0.25 * slope_buf[p, at, lanes]
                    sec_ref[p, at, lanes] = s
                    totals[p * 8 + b] = totals[p * 8 + b] + s * kr
                    w = s * kap_cols[b]
                    along = w if along is None else along + w
                col_part[p, at, :] = along
            return tuple(totals)

        totals = lax.fori_loop(0, rows // 8, group, totals, unroll=2 if rows % 16 == 0 else 1)
        if hi % LANES == 0:
            half = pl.ds(hi - LANES, LANES)
            for p in range(2):
                along = jnp.sum(col_part[p, half, :].T, axis=0, keepdims=True)
                for c in range(2):
                    sums_ref[pl.ds(p, 1), pl.ds(1024 + c * 256 + hi - LANES, LANES)] = jnp.where(
                        core == c, along, 0.0
                    )
    for p in range(2):
        for b in range(8):
            total = jnp.sum(totals[p * 8 + b], axis=0, keepdims=True)
            sums_ref[pl.ds(p, 1), pl.ds(b * LANES, LANES)] = total
    for copy in late:
        copy.wait()


def split(x):
    high = x.astype(jnp.bfloat16)
    return high, (x - high.astype(jnp.float32)).astype(jnp.bfloat16)


def table(lower):
    a = lax.broadcasted_iota(jnp.int32, (BLOCK, BLOCK), 0)
    b = lax.broadcasted_iota(jnp.int32, (BLOCK, BLOCK), 1)
    before = (b < a) if lower else (a < b)
    return jnp.where(before, 1.0, jnp.where(a == b, 0.5, 0.0)).astype(jnp.bfloat16)


def matmul(a, b):
    return jnp.dot(a, b, preferred_element_type=jnp.float32)


def twice(x):
    return jnp.concatenate([x, x], axis=1)


def along_lanes(ref, first):
    return jnp.concatenate([ref[pl.ds(first, 1), :], ref[pl.ds(first + 1, 1), :]], axis=1)


def rows_kernel(rho_ref, sec_ref, kap_rows, kappa_ref, detune_ref, pump_ref, base_ref, rho_out):
    row, col = spot()
    rho_re, rho_im = rho_ref[0], rho_ref[1]
    rho_out[0] = jnp.full((8, LANES), rho_re)
    rho_out[1] = jnp.full((8, LANES), rho_im)
    e, f = 1.0 - rho_re, -rho_im
    kr = twice(kap_rows[...])
    dr = twice(down_rows(detune_ref, row))
    pr = twice(down_rows(pump_ref, row))
    mre_r = (0.5 * rho_re) * kr * kr
    mim_r = (0.5 * rho_im) * kr * kr - dr
    lower = table(True)
    for b in range(1024 // BLOCK):
        lanes = pl.ds(b * BLOCK, BLOCK)
        kc = along_lanes(kappa_ref, col * 8 + 2 * b)
        dc = along_lanes(detune_ref, col * 8 + 2 * b)
        q = []
        for p in range(2):
            high, low = split(sec_ref[p, :, lanes] * kr)
            q.append(matmul(lower, high) + matmul(lower, low))
        s_re, s_im = sec_ref[0, :, lanes], sec_ref[1, :, lanes]
        m_re = mre_r + (0.5 * rho_re) * kc * kc
        m_im = mim_r + (dc - (0.5 * rho_im) * kc * kc)
        i = lax.broadcasted_iota(jnp.int32, (256, BLOCK), 0) + row * 256
        k = lax.broadcasted_iota(jnp.int32, (256, BLOCK), 1) + (col * 1024 + b * BLOCK)
        base_ref[0, :, lanes] = (
            m_re * s_re - m_im * s_im - kr * (e * q[0] - f * q[1]) + jnp.where(i == k, pr, 0.0)
        )
        base_ref[1, :, lanes] = m_re * s_im + m_im * s_re - kr * (e * q[1] + f * q[0])


def cols_kernel(rho_ref, sec_ref, kappa_ref, part_ref, base_ref):
    _, col = spot()
    e, f = 1.0 - rho_ref[0], rho_ref[1]
    upper = table(False)
    carry = [jnp.zeros((256, 1), jnp.float32) for _ in range(2)]
    for b in range(1024 // BLOCK):
        lanes = pl.ds(b * BLOCK, BLOCK)
        kc = along_lanes(kappa_ref, col * 8 + 2 * b)
        q = []
        for p in range(2):
            w = sec_ref[p, :, lanes] * kc
            high, low = split(w)
            q.append(matmul(high, upper) + matmul(low, upper) + carry[p])
            carry[p] = carry[p] + jnp.sum(w, axis=1, keepdims=True)
        base_ref[0, :, lanes] = part_ref[0, :, lanes] - kc * (e * q[0] - f * q[1])
        base_ref[1, :, lanes] = part_ref[1, :, lanes] - kc * (e * q[1] + f * q[0])


def carried(rho_ref, b, a, sign, height):
    rho_re, rho_im = rho_ref[0, 0:1, :], sign * rho_ref[1, 0:1, :]
    both = b[0:1] + (rho_re * a[0:1] - rho_im * a[1:2]), b[1:2] + (rho_re * a[1:2] + rho_im * a[0:1])
    return [jnp.broadcast_to(x, (height, LANES)) for x in both]


OUT_EDGES = (0, 32, 64, 128, 192, 224, 256)


def last_kernel(
    rho_ref, kappa_ref, kap_rows, base_ref, before_ref, after_ref, got_ref, own_ref, theirs_ref,
    out_hbm, out_buf, col_d, sems,
):
    _, col = spot()
    odd = lax.axis_index("core") == 1

    def turn_cols(half):
        at = pl.ds(half * LANES, LANES)
        there = pl.ds(256 + half * LANES, LANES)
        before = jnp.where(odd, got_ref[0, :, there], before_ref[:, at])
        after = jnp.where(odd, got_ref[1, :, there], after_ref[:, at])
        own = jnp.where(
            odd,
            own_ref[:, pl.ds(1280 + half * LANES, LANES)],
            own_ref[:, pl.ds(1024 + half * LANES, LANES)],
        )
        for p, x in enumerate(carried(rho_ref, before, after + own, -1.0, LANES)):
            col_d[p, at, :] = x.T

    turn_cols(0)
    kap_cols = [
        jnp.broadcast_to(kappa_ref[pl.ds(col * 8 + b, 1), :], (8, LANES)) for b in range(8)
    ]
    row_ds = []
    for b in range(8):
        at = pl.ds(b * LANES, LANES)
        theirs = theirs_ref[:, at]
        before, after = put(
            jnp.where(odd, before_ref[:, at], got_ref[0, :, at]),
            jnp.where(odd, after_ref[:, at], got_ref[1, :, at]),
            odd,
            theirs,
        )
        row_ds.append(carried(rho_ref, before, after + own_ref[:, at], 1.0, 8))
    copies = []
    for c, (lo, hi) in enumerate(zip(OUT_EDGES, OUT_EDGES[1:])):
        if lo == LANES:
            turn_cols(1)

        def group(g, carry):
            at = pl.ds(pl.multiple_of(lo + g * 8, 8), 8)
            kr = kap_rows[at, :]
            for p in range(2):
                dc = col_d[p, at, :]
                for b in range(8):
                    lanes = pl.ds(b * LANES, LANES)
                    out_buf[p, at, lanes] = base_ref[p, at, lanes] - (
                        kr * row_ds[b][p] + kap_cols[b] * dc
                    )
            return carry

        lax.fori_loop(0, (hi - lo) // 8, group, 0, unroll=2)
        part = pl.ds(lo, hi - lo)
        copy = pltpu.make_async_copy(out_buf.at[:, part], out_hbm.at[:, part], sems.at[c])
        copy.start()
        copies.append(copy)
    for copy in copies:
        copy.wait()


VM = pl.BlockSpec(memory_space=pltpu.VMEM)
SM = pl.BlockSpec(memory_space=pltpu.SMEM)
HB = pl.BlockSpec(memory_space=pltpu.HBM)
F32 = jnp.float32


def call(kernel, outs, ins, out_specs, scratch=(), alias={}, flops=0, limit=20):
    return pl.pallas_call(
        kernel,
        out_shape=outs,
        in_specs=ins,
        out_specs=out_specs,
        scratch_shapes=list(scratch),
        input_output_aliases=alias,
        cost_estimate=pl.CostEstimate(flops=flops, bytes_accessed=6 * MIB, transcendentals=0),
        compiler_params=pltpu.CompilerParams(vmem_limit_bytes=limit * MIB),
    )


def vmem(*shape):
    return pltpu.VMEM(shape, F32)


WHOLE = (2, 256, 1024)
DMA = pltpu.SemaphoreType.DMA


def sums(corr, slope, *small):
    return call(
        sums_kernel,
        [vmem(*WHOLE), vmem(2, 2048), vmem(256, 128)] + [vmem(64, 128)] * 3 + [vmem(7, 2, 1024)],
        [HB] * 5,
        [VM] * 7,
        [vmem(*WHOLE), vmem(*WHOLE), vmem(2, 256, 128), DMA((2, len(PIECES))), DMA((3,))],
    )(corr, slope, *small)


def rows_part(rho, sec, kap_rows, *small):
    return call(
        rows_kernel, [vmem(*WHOLE), vmem(2, 8, 128)], [SM] + [VM] * 5, [VM] * 2, flops=10**9
    )(rho, sec, kap_rows, *small)


def cols_part(rho, sec, kappa, part):
    return call(cols_kernel, vmem(*WHOLE), [SM] + [VM] * 3, VM, alias={3: 0}, flops=10**9)(
        rho, sec, kappa, part
    )


def last(*operands):
    return call(
        last_kernel,
        jax.ShapeDtypeStruct(WHOLE, F32),
        [VM] * 9,
        HB,
        [vmem(*WHOLE), vmem(2, 256, 128), DMA((len(OUT_EDGES) - 1,))],
    )(*operands)


def put(before, after, lower, x):
    return before + jnp.where(lower, x, 0.0), after + jnp.where(lower, 0.0, x)


def shards(corr, slope_prev, kappa, detuning, pump, rho):
    small = (v.reshape(64, 128) for v in (kappa, detuning, pump))
    held = (pltpu.with_memory_space_constraint(v, pltpu.HBM) for v in (corr, slope_prev, *small))
    sec, own, kap_rows, kappa, detune, pump, places = sums(*held)
    odd, lower1, lower2, far1, far2, xh_first, xl_last = (place > 0.5 for place in places)
    tie = lax.optimization_barrier
    other_core = {"core": across}

    theirs = exchange(own, other_core, other_core)
    chip = own + theirs
    mine = jnp.where(odd, chip[:, :1024], chip[:, 1024:])
    mine, sec = tie((mine, sec))
    got = exchange(mine, {"z": across}, {"y": across})
    base, rhos = rows_part(rho, sec, kap_rows, kappa, detune, pump)
    zero = jnp.zeros_like(mine)
    before, after = put(zero, zero, lower1, got)
    pair = mine + got
    pair, base = tie((pair, base))
    got = exchange(pair, {"z": z_next}, {"y": y_next})
    got, base = tie((got, base))
    base = cols_part(rho, sec, kappa, base)
    before, after = put(before, after, lower2, got)
    far = put(zero, zero, far1, pair)
    far = put(*far, far2, got)
    near = put(before, after, xh_first, mine)
    there = jnp.stack([jnp.where(odd, f, n) for f, n in zip(far, near)])
    got = exchange(there, {"z": z_far}, {"xh": across})
    before, after = before + got[0], after + got[1]
    line, base = tie((mine + before + after, base))
    got = exchange(line, {"xl": across}, None)
    before, after = put(before, after, xl_last, got)
    got = exchange(jnp.stack([before, after]), other_core, other_core)
    return last(rhos, kappa, kap_rows, base, before, after, got, own, theirs)


def solution(mesh):
    fine = Mesh(mesh.devices.reshape(SIZES), AXES)
    placed = P(None, ROW, COL)
    return jax.shard_map(
        shards,
        mesh=fine,
        in_specs=(placed, placed, P(), P(), P(), P()),
        out_specs=placed,
        check_vma=False,
    )
```
